32 devices in a mesh: rad: 4 (over x, core), col: 8 (over z, y).
Axes of the slice: x: 2, y: 2, z: 4, core: 2. Of those that a mesh axis runs over, the one named last changes fastest.
Arguments:
- cotangent: float32 [512, 3, 128, 256], P('rad', None, 'col'), may hold values from -6 to 6
- state_axial: float32 [512, 128, 256], P('rad', 'col'), may hold values from -6 to 6
- helm_inverse: float32 [3, 512, 512], P(None, None, 'rad'), as said below
- rotation_rate: float32 [512], P('rad'), may hold values from 0.5 to 2
Outputs:
- gradient: float32 [512, 3, 128, 256], P('rad', None, 'col')
The draws below stay inside these ranges and needn't reach their ends.
Inputs may be any that keep to these rules, and one draw needn't show every extreme that they name: `helm_inverse`: entries of every matrix lie between -1 and 2.
All inputs are finite; a program needn't handle non-finite values.
Results may differ from the reference program's by a relative error of at most 0.00018.
Values sent between devices are 32-bit elements; how exact they have to be, the bound alone decides.
No kernel may reach another device: no remote copies, remote signals or barrier semaphores. Data moves between devices by JAX's collectives and lax.ppermute only.
A program may use at most 128 MiB of HBM per device.

```python
import math
import jax
import jax.numpy as jnp
from jax import lax

NR = 512
NPHI = 256
SECTIONS = 2
NZ = 128


def draw_helm_inverse(key, part):
    offdiag = jax.random.truncated_normal(key, -4.0, 4.0, (3, NR, NR), jnp.float32) * (0.5 / math.sqrt(NR))
    return jnp.eye(NR, dtype=jnp.float32)[None] + offdiag


def levels(key, dims, shards, smallest, top_value):
    def one(position, parts):
        steps = jax.random.uniform(jax.random.fold_in(jax.random.fold_in(key, 6), position), (parts,), jnp.float32, smallest / len(shards), top_value / len(shards))
        return jnp.repeat(jnp.exp(steps), dims[position] // parts).reshape((-1,) + (1,) * (len(dims) - position - 1))

    level = one(*shards[0])
    for cut in shards[1:]:
        level = level * one(*cut)
    return level


def bell_draw(rng, dims, scale, limit, shards=(), kind=jnp.bfloat16):
    drawn = scale * jax.random.normal(rng, dims, jnp.float32)
    if shards:
        drawn = drawn * levels(rng, dims, shards, -0.22, 0.18)
    return jnp.clip(drawn, -limit, limit).astype(kind)


def setup_inputs(seed: int = 0) -> dict:
    streams_of = jax.random.split(jax.random.key(seed), 5)
    return {
        "cotangent": bell_draw(streams_of[0], (NR, 3, NZ, NPHI), 1.0, 6.0, ((0, 4), (2, 8)), jnp.float32),
        "state_axial": bell_draw(streams_of[1], (NR, NZ, NPHI), 1.0, 6.0, ((0, 4), (1, 8)), jnp.float32),
        "helm_inverse": draw_helm_inverse(jax.random.fold_in(streams_of[4], 71), 0),
        "rotation_rate": jnp.clip(jnp.exp(math.log(2.0) - 1.3862944 * jax.random.uniform(streams_of[3], (NR,), jnp.float32) ** levels(streams_of[3], (NR,), ((0, 4),), -0.2, 0.2)), 0.5, 2.0),
    }


def axial_adjoint(current, state_axial, rotation_rate):
    upper = jnp.roll(current, -1, axis=2)
    lower = jnp.roll(current, 1, axis=2)
    laplace = upper - 2.0 * current + lower
    transport = state_axial[:, None] * (lower - upper)
    rate = rotation_rate[:, None, None]
    turning = jnp.stack((rate * current[:, 1], -rate * current[:, 0], jnp.zeros_like(current[:, 2])), axis=1)
    return current + 0.2 * laplace + 0.15 * transport + 0.25 * turning


def reference(cotangent, state_axial, helm_inverse, rotation_rate):
    current = cotangent
    for section_index in range(SECTIONS):
        stenciled = axial_adjoint(current, state_axial, rotation_rate)
        pieces = []
        for component in range(3):
            flat = stenciled[:, component].reshape(NR, NZ * NPHI)
            mapped = jnp.dot(helm_inverse[component].T, flat, precision=lax.Precision.HIGHEST)
            pieces.append(mapped.reshape(NR, NZ, NPHI))
        current = jnp.stack(pieces, axis=1)
    return current
```

```python
import jax
import jax.numpy as jnp
from jax import lax
from jax.experimental import pallas as pl
from jax.experimental.pallas import tpu as pltpu
from jax.sharding import PartitionSpec as P

SECTIONS = 2
CHUNKS = 4

diffusion_coeff = 0.2
advection_coeff = 0.15
rotation_coeff = 0.25

F32 = jnp.float32
BF16 = jnp.bfloat16
MB = 1 << 20


def shape(dims, dtype=F32):
    return jax.ShapeDtypeStruct(dims, dtype)


def cost(flops, moved):
    return pl.CostEstimate(flops=int(flops), bytes_accessed=int(moved), transcendentals=0)


def params(limit=40):
    return pltpu.CompilerParams(vmem_limit_bytes=limit * MB)


def stencil(cur, upper, lower, other, state):
    up = diffusion_coeff - advection_coeff * state
    down = diffusion_coeff + advection_coeff * state
    out = (1.0 - 2.0 * diffusion_coeff) * cur + up * upper + down * lower
    return out if other is None else out + other


def split(values):
    high = values.astype(BF16)
    return high, (values - high.astype(F32)).astype(BF16)


def product(x_parts, h_high, h_low):
    pairs = [split(x) for x in x_parts]
    high = jnp.concatenate([p[0] for p in pairs], axis=1)
    low = jnp.concatenate([p[1] for p in pairs], axis=1)

    def dot(a, b):
        return jnp.dot(a, b, preferred_element_type=F32)

    return dot(high, h_high) + (dot(high, h_low) + dot(low, h_high))


def state_kernel(where, state, rate, out, *, modes, nz):
    width = state.shape[1]
    for z in range(nz):
        out[z * width : (z + 1) * width, :] = state[pl.ds(z, modes, stride=nz), :].T
    if out.shape[0] > nz * width:
        out[nz * width :, :] = jnp.broadcast_to(rate[...], (out.shape[0] - nz * width, modes))


def turn_state(where, state, rate, foreign, extra):
    modes, nz, nphi = state.shape
    half = nphi // 2
    side = (lambda i, w: (0, 1 - (w[0] >> 1))) if foreign else (lambda i, w: (0, w[0] >> 1))
    rows = nz * half + extra
    return pl.pallas_call(
        lambda *refs: state_kernel(*refs, modes=modes, nz=nz),
        out_shape=shape((rows, modes)),
        grid_spec=pltpu.PrefetchScalarGridSpec(
            num_scalar_prefetch=1,
            grid=(1,),
            in_specs=[pl.BlockSpec((modes * nz, half), side), pl.BlockSpec((1, modes), lambda i, w: (0, 0))],
            out_specs=pl.BlockSpec((rows, modes), lambda i, w: (0, 0)),
        ),
        compiler_params=params(16),
        cost_estimate=cost(rows * modes, 8 * rows * modes),
        name="turn_state",
    )(where, state.reshape(modes * nz, nphi), rate)


def first_kernel(where, cot, state, after, before, rate, *rest, modes, nz, chunks):
    outs, turned = rest[:-1], rest[-1]
    half = cot.shape[1]
    width = half // chunks
    for c in range(3):
        turned[c, 0] = before[c * modes : (c + 1) * modes, :].T
        for z in range(nz):
            turned[c, z + 1] = cot[pl.ds(c * nz + z, modes, stride=3 * nz), :].T
        turned[c, nz + 1] = after[c * modes : (c + 1) * modes, :].T
    turn = rotation_coeff * rate[...]
    for z in range(nz):
        for k in range(chunks):
            at = slice(k * width, (k + 1) * width)
            st = state[z * half + k * width : z * half + (k + 1) * width, :]
            cur = [turned[c, z + 1, at, :] for c in range(3)]
            others = (turn * cur[1], -turn * cur[0], None)
            for c in range(3):
                outs[k][c, z] = stencil(cur[c], turned[c, z + 2, at, :], turned[c, z, at, :], others[c], st)


def first_stencil(where, cot, state_turned, after, before, rate, foreign, chunks):
    modes, comps, nz, nphi = cot.shape
    half = nphi // 2
    side = (lambda i, w: (0, 1 - (w[0] >> 1))) if foreign else (lambda i, w: (0, w[0] >> 1))
    whole = lambda i, w: (0, 0)
    out = (comps, nz, half // chunks, modes)
    return pl.pallas_call(
        lambda *refs: first_kernel(*refs, modes=modes, nz=nz, chunks=chunks),
        out_shape=[shape(out)] * chunks,
        grid_spec=pltpu.PrefetchScalarGridSpec(
            num_scalar_prefetch=1,
            grid=(1,),
            in_specs=[
                pl.BlockSpec((modes * comps * nz, half), side),
                pl.BlockSpec((nz * half, modes), whole),
                pl.BlockSpec((comps * modes, half), side),
                pl.BlockSpec((comps * modes, half), side),
                pl.BlockSpec((1, modes), whole),
            ],
            out_specs=[pl.BlockSpec(out, lambda i, w: (0, 0, 0, 0))] * chunks,
            scratch_shapes=[pltpu.VMEM((comps, nz + 2, half, modes), F32)],
        ),
        compiler_params=params(32),
        cost_estimate=cost(12 * modes * comps * nz * half, 8 * modes * comps * nz * half),
        name="first_stencil",
    )(where, cot.reshape(modes * comps * nz, nphi), state_turned, after, before, rate)


def helm_kernel(where, own, far, high, low):
    for g, part in enumerate((own, far)):
        h, l = split(part[...])
        cols = slice(g * part.shape[2], (g + 1) * part.shape[2])
        high[:, :, cols] = h
        low[:, :, cols] = l


def split_helm(where, own, far):
    comps, rows, modes = own.shape
    block = lambda k, w: (0, w[0] ^ (((k & 1) << 1) | (k >> 1)), 0)
    out = (comps, rows, 2 * modes)
    return pl.pallas_call(
        helm_kernel,
        out_shape=[shape(out, BF16)] * 2,
        grid_spec=pltpu.PrefetchScalarGridSpec(
            num_scalar_prefetch=1,
            grid=(rows // modes,),
            in_specs=[pl.BlockSpec((comps, modes, modes), block)] * 2,
            out_specs=[pl.BlockSpec((comps, modes, 2 * modes), lambda k, w: (0, k, 0))] * 2,
        ),
        compiler_params=params(16),
        cost_estimate=cost(4 * comps * rows * modes, 16 * comps * rows * modes),
        name="split_helm",
    )(where, own, far)


def map1_kernel(own, far, own_peer, far_peer, high, low, out, first, last):
    _, nz, width, modes = own.shape
    rows = nz * width
    parts = [ref[0].reshape(rows, modes) for ref in (own, far, own_peer, far_peer)]
    res = product(parts, high[0], low[0]).reshape(nz, width, high.shape[2])
    out[0] = res
    first[0] = res[0]
    last[0] = res[nz - 1]


def map1(own, far, own_peer, far_peer, high, low, k):
    comps, nz, width, modes = far.shape
    rows, cols = high.shape[1:]
    here = pl.BlockSpec((1, nz, width, modes), lambda c: (c, 0, k, 0))
    chunk = pl.BlockSpec((1, nz, width, modes), lambda c: (c, 0, 0, 0))
    helm = pl.BlockSpec((1, rows, cols), lambda c: (c, 0, 0))
    layer = pl.BlockSpec((1, width, cols), lambda c: (c, 0, 0))
    return pl.pallas_call(
        map1_kernel,
        out_shape=[shape((comps, nz, width, cols)), shape((comps, width, cols)), shape((comps, width, cols))],
        grid=(comps,),
        in_specs=[here, chunk, here, chunk, helm, helm],
        out_specs=[pl.BlockSpec((1, nz, width, cols), lambda c: (c, 0, 0, 0)), layer, layer],
        compiler_params=params(24),
        cost_estimate=cost(6 * comps * nz * width * rows * cols, 4 * comps * (nz * width * (rows + cols) + rows * cols)),
        name=f"map1_{k}",
    )(own, far, own_peer, far_peer, high, low)


def second_kernel(cur, after, before, state_own, state_far, rate, out, *, k, half):
    comps, nz, width, cols = cur.shape
    modes = cols // 2
    rates = (rate[...], state_far[nz * half : nz * half + 1, :])
    for g in range(2):
        lanes = slice(g * modes, (g + 1) * modes)
        turn = rotation_coeff * rates[g]
        state = (state_own, state_far)[g]
        for z in range(nz):
            st = state[z * half + k * width : z * half + (k + 1) * width, :]
            here = [cur[c, z, :, lanes] for c in range(comps)]
            others = (turn * here[1], -turn * here[0], None)
            for c in range(comps):
                upper = cur[c, z + 1, :, lanes] if z + 1 < nz else after[c, :, lanes]
                lower = cur[c, z - 1, :, lanes] if z else before[c, :, lanes]
                out[c, z, :, lanes] = stencil(here[c], upper, lower, others[c], st)


def second_stencil(cur, after, before, state_own, state_far, rate, k, half):
    return pl.pallas_call(
        lambda *refs: second_kernel(*refs, k=k, half=half),
        out_shape=shape(cur.shape),
        compiler_params=params(16),
        cost_estimate=cost(12 * cur.size, 8 * cur.size),
        name=f"second_stencil_{k}",
    )(cur, after, before, state_own, state_far, rate)


def map2_kernel(own, peer, high, low, out_own, out_far):
    _, nz, width, cols = own.shape
    parts = [ref[0].reshape(nz * width, cols) for ref in (own, peer)]
    res = product(parts, high[0], low[0]).reshape(nz, width, cols)
    out_own[0] = res[:, :, : cols // 2]
    out_far[0] = res[:, :, cols // 2 :]


def map2(own, peer, high, low, k):
    comps, nz, width, cols = own.shape
    rows = high.shape[1]
    chunk = pl.BlockSpec((1, nz, width, cols), lambda c: (c, 0, 0, 0))
    helm = pl.BlockSpec((1, rows, cols), lambda c: (c, 0, 0))
    out = (comps, nz, width, cols // 2)
    return pl.pallas_call(
        map2_kernel,
        out_shape=[shape(out)] * 2,
        grid=(comps,),
        in_specs=[chunk, chunk, helm, helm],
        out_specs=[pl.BlockSpec((1, nz, width, cols // 2), lambda c: (c, 0, 0, 0))] * 2,
        compiler_params=params(24),
        cost_estimate=cost(6 * comps * nz * width * rows * cols, 4 * comps * (nz * width * (rows + cols) + rows * cols)),
        name=f"map2_{k}",
    )(own, peer, high, low)


def last_kernel(where, *refs, nz, chunks, extra):
    ins, out = refs[:chunks], refs[-1]
    width, modes = ins[0].shape[2:]
    for c in range(ins[0].shape[0]):
        for z in range(nz):
            whole = jnp.concatenate([ref[c, z] for ref in ins], axis=0)
            out[pl.ds(c * nz + z, modes, stride=3 * nz), :] = whole.T


def write_half(where, pieces, nphi, foreign, base=None):
    comps, nz, width, modes = pieces[0].shape
    chunks = len(pieces)
    side = (lambda i, w: (0, 1 - (w[0] >> 1))) if foreign else (lambda i, w: (0, w[0] >> 1))
    rows = modes * comps * nz
    extra = () if base is None else (base,)
    return pl.pallas_call(
        lambda *refs: last_kernel(*refs, nz=nz, chunks=chunks, extra=len(extra)),
        out_shape=shape((rows, nphi)),
        grid_spec=pltpu.PrefetchScalarGridSpec(
            num_scalar_prefetch=1,
            grid=(1,),
            in_specs=[pl.BlockSpec(p.shape, lambda i, w: (0, 0, 0, 0)) for p in pieces]
            + [pl.BlockSpec(memory_space=pl.ANY)] * len(extra),
            out_specs=pl.BlockSpec((rows, nphi // 2), side),
        ),
        input_output_aliases={1 + chunks: 0} if extra else {},
        compiler_params=params(24),
        cost_estimate=cost(rows * nphi, 4 * rows * nphi),
        name="write_foreign" if foreign else "write_own",
    )(where, *pieces, *extra)


def on_device(cotangent, state_axial, helm_inverse, rotation_rate):
    modes, comps, nz, nphi = cotangent.shape
    half = nphi // 2
    peers, cols = lax.axis_size("rad"), lax.axis_size("col")
    up = [(i, (i + 1) % cols) for i in range(cols)]
    down = [(j, i) for i, j in up]

    def across(array):
        return lax.ppermute(array, "rad", [(i, i ^ 2) for i in range(peers)])

    def beside(array):
        return lax.ppermute(array, "rad", [(i, i ^ 1) for i in range(peers)])

    where = lax.axis_index("rad").astype(jnp.int32).reshape(1)
    rate = rotation_rate.reshape(1, modes)

    helm_far = across(helm_inverse)
    state_foreign = turn_state(where, state_axial, rate, True, 8)
    state_far = across(state_foreign)
    leading = jnp.transpose(cotangent[:, :, 0], (1, 0, 2)).reshape(comps * modes, nphi)
    last = jnp.transpose(cotangent[:, :, nz - 1], (1, 0, 2)).reshape(comps * modes, nphi)
    before = lax.ppermute(last, "col", up)
    after = lax.ppermute(leading, "col", down)
    state_own = turn_state(where, state_axial, rate, False, 0)

    sent = first_stencil(where, cotangent, state_foreign, after, before, rate, True, CHUNKS)
    far = [across(s) for s in sent]
    (own,) = first_stencil(where, cotangent, state_own, after, before, rate, False, 1)
    own_peer = beside(own)
    high, low = split_helm(where, helm_inverse, helm_far)

    kept, back = [], []
    for k in range(CHUNKS):
        cur, leading, last = map1(own, far[k], own_peer, beside(far[k]), high, low, k)
        before = lax.ppermute(last, "col", up)
        after = lax.ppermute(leading, "col", down)
        nxt = second_stencil(cur, after, before, state_own, state_far, rate, k, half)
        mine, theirs = map2(nxt, beside(nxt), high, low, k)
        kept.append(mine)
        back.append(across(theirs))
    out = write_half(where, kept, nphi, False)
    out = write_half(where, back, nphi, True, out)
    return out.reshape(modes, comps, nz, nphi)


def solution(mesh):
    in_specs = (P("rad", None, "col", None), P("rad", "col", None), P(None, None, "rad"), P("rad"))
    out_specs = P("rad", None, "col", None)
    return jax.shard_map(
        on_device, mesh=mesh, in_specs=in_specs, out_specs=out_specs, check_vma=False
    )
```

```python
import jax
import jax.numpy as jnp
from jax import lax
from jax.experimental import pallas as pl
from jax.experimental.pallas import tpu as pltpu
from jax.sharding import PartitionSpec as P

SECTIONS = 2
CHUNKS = 4
PIECES = 4

diffusion_coeff = 0.2
advection_coeff = 0.15
rotation_coeff = 0.25

F32 = jnp.float32
BF16 = jnp.bfloat16
MB = 1 << 20


def shape(dims, dtype=F32):
    return jax.ShapeDtypeStruct(dims, dtype)


def cost(flops, moved):
    return pl.CostEstimate(flops=int(flops), bytes_accessed=int(moved), transcendentals=0)


def params(limit=40):
    return pltpu.CompilerParams(vmem_limit_bytes=limit * MB)


def stencil(cur, upper, lower, other, state):
    up = diffusion_coeff - advection_coeff * state
    down = diffusion_coeff + advection_coeff * state
    out = (1.0 - 2.0 * diffusion_coeff) * cur + up * upper + down * lower
    return out if other is None else out + other


def split(values):
    high = values.astype(BF16)
    return high, (values - high.astype(F32)).astype(BF16)


def product(x_parts, h_high, h_low):
    pairs = [split(x) for x in x_parts]
    high = jnp.concatenate([p[0] for p in pairs], axis=1)
    low = jnp.concatenate([p[1] for p in pairs], axis=1)

    def dot(a, b):
        return jnp.dot(a, b, preferred_element_type=F32)

    return dot(high, h_high) + (dot(high, h_low) + dot(low, h_high))


def state_kernel(where, state, rate, out, *, modes, nz):
    width = state.shape[1]
    for z in range(nz):
        out[z * width : (z + 1) * width, :] = state[pl.ds(z, modes, stride=nz), :].T
    if out.shape[0] > nz * width:
        out[nz * width :, :] = jnp.broadcast_to(rate[...], (out.shape[0] - nz * width, modes))


def turn_state(where, state, rate, foreign, extra):
    modes, nz, nphi = state.shape
    half = nphi // 2
    side = (lambda i, w: (0, 1 - (w[0] >> 1))) if foreign else (lambda i, w: (0, w[0] >> 1))
    rows = nz * half + extra
    return pl.pallas_call(
        lambda *refs: state_kernel(*refs, modes=modes, nz=nz),
        out_shape=shape((rows, modes)),
        grid_spec=pltpu.PrefetchScalarGridSpec(
            num_scalar_prefetch=1,
            grid=(1,),
            in_specs=[pl.BlockSpec((modes * nz, half), side), pl.BlockSpec((1, modes), lambda i, w: (0, 0))],
            out_specs=pl.BlockSpec((rows, modes), lambda i, w: (0, 0)),
        ),
        compiler_params=params(16),
        cost_estimate=cost(rows * modes, 8 * rows * modes),
        name="turn_state",
    )(where, state.reshape(modes * nz, nphi), rate)


def edge_kernel(cot, leading, last, *, modes, nz):
    for c in range(3):
        at = slice(c * modes, (c + 1) * modes)
        leading[at, :] = cot[pl.ds(c * nz, modes, stride=3 * nz), :]
        last[at, :] = cot[pl.ds(c * nz + nz - 1, modes, stride=3 * nz), :]


def edge_layers(cot):
    modes, comps, nz, nphi = cot.shape
    return pl.pallas_call(
        lambda *refs: edge_kernel(*refs, modes=modes, nz=nz),
        out_shape=[shape((comps * modes, nphi))] * 2,
        grid=(2,),
        in_specs=[pl.BlockSpec((modes * comps * nz, nphi // 2), lambda h: (0, h))],
        out_specs=[pl.BlockSpec((comps * modes, nphi // 2), lambda h: (0, h))] * 2,
        compiler_params=params(16),
        cost_estimate=cost(modes * comps * nphi, 16 * modes * comps * nphi),
        name="edge_layers",
    )(cot.reshape(modes * comps * nz, nphi))


def first_kernel(where, cot, state, after, before, rate, *rest, modes, nz, chunks):
    outs, turned = rest[:-1], rest[-1]
    half = cot.shape[1]
    width = half // chunks
    for c in range(3):
        turned[c, 0] = before[c * modes : (c + 1) * modes, :].T
        for z in range(nz):
            turned[c, z + 1] = cot[pl.ds(c * nz + z, modes, stride=3 * nz), :].T
        turned[c, nz + 1] = after[c * modes : (c + 1) * modes, :].T
    turn = rotation_coeff * rate[...]
    for z in range(nz):
        for k in range(chunks):
            at = slice(k * width, (k + 1) * width)
            st = state[z * half + k * width : z * half + (k + 1) * width, :]
            cur = [turned[c, z + 1, at, :] for c in range(3)]
            others = (turn * cur[1], -turn * cur[0], None)
            for c in range(3):
                outs[k][c, z] = stencil(cur[c], turned[c, z + 2, at, :], turned[c, z, at, :], others[c], st)


def first_stencil(where, cot, state_turned, after, before, rate, foreign, chunks):
    modes, comps, nz, nphi = cot.shape
    half = nphi // 2
    side = (lambda i, w: (0, 1 - (w[0] >> 1))) if foreign else (lambda i, w: (0, w[0] >> 1))
    whole = lambda i, w: (0, 0)
    out = (comps, nz, half // chunks, modes)
    return pl.pallas_call(
        lambda *refs: first_kernel(*refs, modes=modes, nz=nz, chunks=chunks),
        out_shape=[shape(out)] * chunks,
        grid_spec=pltpu.PrefetchScalarGridSpec(
            num_scalar_prefetch=1,
            grid=(1,),
            in_specs=[
                pl.BlockSpec((modes * comps * nz, half), side),
                pl.BlockSpec((nz * half, modes), whole),
                pl.BlockSpec((comps * modes, half), side),
                pl.BlockSpec((comps * modes, half), side),
                pl.BlockSpec((1, modes), whole),
            ],
            out_specs=[pl.BlockSpec(out, lambda i, w: (0, 0, 0, 0))] * chunks,
            scratch_shapes=[pltpu.VMEM((comps, nz + 2, half, modes), F32)],
        ),
        compiler_params=params(32),
        cost_estimate=cost(12 * modes * comps * nz * half, 8 * modes * comps * nz * half),
        name="first_stencil",
    )(where, cot.reshape(modes * comps * nz, nphi), state_turned, after, before, rate)


def helm_kernel(where, own, far, high, low):
    for g, part in enumerate((own[...], far[0])):
        h, l = split(part)
        cols = slice(g * part.shape[2], (g + 1) * part.shape[2])
        high[:, :, cols] = h
        low[:, :, cols] = l


def split_helm(where, own, far):
    comps, rows, modes = own.shape
    block = lambda k, w: w[0] ^ (((k & 1) << 1) | (k >> 1))
    out = (comps, rows, 2 * modes)
    return pl.pallas_call(
        helm_kernel,
        out_shape=[shape(out, BF16)] * 2,
        grid_spec=pltpu.PrefetchScalarGridSpec(
            num_scalar_prefetch=1,
            grid=(rows // modes,),
            in_specs=[
                pl.BlockSpec((comps, modes, modes), lambda k, w: (0, block(k, w), 0)),
                pl.BlockSpec((1, comps, modes, modes), lambda k, w: (block(k, w) ^ w[1], 0, 0, 0)),
            ],
            out_specs=[pl.BlockSpec((comps, modes, 2 * modes), lambda k, w: (0, k, 0))] * 2,
        ),
        compiler_params=params(16),
        cost_estimate=cost(4 * comps * rows * modes, 16 * comps * rows * modes),
        name="split_helm",
    )(where, own, far)


def map1_kernel(own, far, own_peer, far_peer, high, low, out, first, last):
    _, nz, width, modes = own.shape
    rows = nz * width
    parts = [ref[0].reshape(rows, modes) for ref in (own, far, own_peer, far_peer)]
    res = product(parts, high[0], low[0]).reshape(nz, width, high.shape[2])
    out[0] = res
    first[0] = res[0]
    last[0] = res[nz - 1]


def map1(own, far, own_peer, far_peer, high, low, k):
    comps, nz, width, modes = far.shape
    rows, cols = high.shape[1:]
    here = pl.BlockSpec((1, nz, width, modes), lambda c: (c, 0, k, 0))
    chunk = pl.BlockSpec((1, nz, width, modes), lambda c: (c, 0, 0, 0))
    helm = pl.BlockSpec((1, rows, cols), lambda c: (c, 0, 0))
    layer = pl.BlockSpec((1, width, cols), lambda c: (c, 0, 0))
    return pl.pallas_call(
        map1_kernel,
        out_shape=[shape((comps, nz, width, cols)), shape((comps, width, cols)), shape((comps, width, cols))],
        grid=(comps,),
        in_specs=[here, chunk, here, chunk, helm, helm],
        out_specs=[pl.BlockSpec((1, nz, width, cols), lambda c: (c, 0, 0, 0)), layer, layer],
        compiler_params=params(24),
        cost_estimate=cost(6 * comps * nz * width * rows * cols, 4 * comps * (nz * width * (rows + cols) + rows * cols)),
        name=f"map1_{k}",
    )(own, far, own_peer, far_peer, high, low)


def second_kernel(cur, after, before, state_own, state_far, rate, out, *, k, half):
    comps, nz, width, cols = cur.shape
    modes = cols // 2
    rates = (rate[...], state_far[nz * half : nz * half + 1, :])
    for g in range(2):
        lanes = slice(g * modes, (g + 1) * modes)
        turn = rotation_coeff * rates[g]
        state = (state_own, state_far)[g]
        for z in range(nz):
            st = state[z * half + k * width : z * half + (k + 1) * width, :]
            here = [cur[c, z, :, lanes] for c in range(comps)]
            others = (turn * here[1], -turn * here[0], None)
            for c in range(comps):
                upper = cur[c, z + 1, :, lanes] if z + 1 < nz else after[c, :, lanes]
                lower = cur[c, z - 1, :, lanes] if z else before[c, :, lanes]
                out[c, z, :, lanes] = stencil(here[c], upper, lower, others[c], st)


def second_stencil(cur, after, before, state_own, state_far, rate, k, half):
    return pl.pallas_call(
        lambda *refs: second_kernel(*refs, k=k, half=half),
        out_shape=shape(cur.shape),
        compiler_params=params(16),
        cost_estimate=cost(12 * cur.size, 8 * cur.size),
        name=f"second_stencil_{k}",
    )(cur, after, before, state_own, state_far, rate)


def map2_kernel(own, peer, high, low, out_own, out_far):
    _, nz, width, cols = own.shape
    parts = [ref[0].reshape(nz * width, cols) for ref in (own, peer)]
    res = product(parts, high[0], low[0]).reshape(nz, width, cols)
    out_own[0] = res[:, :, : cols // 2]
    out_far[0] = res[:, :, cols // 2 :]


def map2(own, peer, high, low, k):
    comps, nz, width, cols = own.shape
    rows = high.shape[1]
    chunk = pl.BlockSpec((1, nz, width, cols), lambda c: (c, 0, 0, 0))
    helm = pl.BlockSpec((1, rows, cols), lambda c: (c, 0, 0))
    out = (comps, nz, width, cols // 2)
    return pl.pallas_call(
        map2_kernel,
        out_shape=[shape(out)] * 2,
        grid=(comps,),
        in_specs=[chunk, chunk, helm, helm],
        out_specs=[pl.BlockSpec((1, nz, width, cols // 2), lambda c: (c, 0, 0, 0))] * 2,
        compiler_params=params(24),
        cost_estimate=cost(6 * comps * nz * width * rows * cols, 4 * comps * (nz * width * (rows + cols) + rows * cols)),
        name=f"map2_{k}",
    )(own, peer, high, low)


def last_kernel(where, *refs, nz, chunks):
    ins, out = refs[:chunks], refs[-1]
    for z in range(nz):
        whole = jnp.concatenate([ref[0, z] for ref in ins], axis=0)
        out[:, z, :] = whole.T


def write_half(where, pieces, nphi, foreign, base=None):
    comps, nz, width, modes = pieces[0].shape
    chunks = len(pieces)
    side = (lambda c, w: (0, c, 1 - (w[0] >> 1))) if foreign else (lambda c, w: (0, c, w[0] >> 1))
    extra = () if base is None else (base,)
    return pl.pallas_call(
        lambda *refs: last_kernel(*refs, nz=nz, chunks=chunks),
        out_shape=shape((modes, comps * nz, nphi)),
        grid_spec=pltpu.PrefetchScalarGridSpec(
            num_scalar_prefetch=1,
            grid=(comps,),
            in_specs=[pl.BlockSpec((1,) + p.shape[1:], lambda c, w: (c, 0, 0, 0)) for p in pieces]
            + [pl.BlockSpec(memory_space=pl.ANY)] * len(extra),
            out_specs=pl.BlockSpec((modes, nz, nphi // 2), side),
        ),
        input_output_aliases={1 + chunks: 0} if extra else {},
        compiler_params=params(24),
        cost_estimate=cost(comps * nz * modes * nphi, 4 * comps * nz * modes * nphi),
        name="write_foreign" if foreign else "write_own",
    )(where, *pieces, *extra)


def tied(value, *others):
    return lax.optimization_barrier((value, *others))[0]


def on_device(cotangent, state_axial, helm_inverse, rotation_rate):
    modes, comps, nz, nphi = cotangent.shape
    half = nphi // 2
    peers, cols = lax.axis_size("rad"), lax.axis_size("col")
    up = [(i, (i + 1) % cols) for i in range(cols)]
    down = [(j, i) for i, j in up]

    def across(array):
        return lax.ppermute(array, "rad", [(i, i ^ 2) for i in range(peers)])

    def beside(array):
        return lax.ppermute(array, "rad", [(i, i ^ 1) for i in range(peers)])

    def hop(array, mask):
        return lax.ppermute(array, "col", [(i, i ^ mask) for i in range(cols)])

    lot = lax.axis_index("col").astype(jnp.int32) & (PIECES - 1)
    where = jnp.stack([lax.axis_index("rad").astype(jnp.int32), lot])
    rate = rotation_rate.reshape(1, modes)

    piece = lax.dynamic_slice_in_dim(helm_inverse, lot * modes, modes, axis=1)
    helm_far = across(piece)[None]
    state_foreign = turn_state(where, state_axial, rate, True, 8)
    state_far = across(state_foreign)
    leading, last = edge_layers(cotangent)
    before = lax.ppermute(last, "col", up)
    after = lax.ppermute(leading, "col", down)
    after = tied(after, helm_far)
    sent = first_stencil(where, cotangent, state_foreign, after, before, rate, True, CHUNKS)
    far = [across(tied(s, state_far) if k else s) for k, s in enumerate(sent)]
    mask = 1
    while mask < PIECES:
        helm_far = jnp.concatenate([helm_far, hop(helm_far, mask)])
        mask *= 2

    state_own = turn_state(where, state_axial, rate, False, 0)
    (own,) = first_stencil(where, cotangent, state_own, after, before, rate, False, 1)
    own_peer = beside(own)
    high, low = split_helm(where, helm_inverse, helm_far)

    once = 1 + (where[0] >> 8)
    kept, back = [], []
    for k in range(CHUNKS):

        def chain(_, pair, k=k):
            here = pair[0]
            cur, leading, last = map1(own, here, own_peer, beside(here), high, low, k)
            before = lax.ppermute(last, "col", up)
            after = lax.ppermute(leading, "col", down)
            nxt = second_stencil(cur, after, before, state_own, state_far, rate, k, half)
            mine, theirs = map2(nxt, beside(nxt), high, low, k)
            return theirs, mine

        here = tied(far[k], kept[-1]) if k else far[k]
        theirs, mine = lax.fori_loop(0, once, chain, (here, sent[k]))
        kept.append(mine)
        back.append(across(theirs))
    out = write_half(where, kept, nphi, False)
    out = write_half(where, back, nphi, True, out)
    return out.reshape(modes, comps, nz, nphi)


def solution(mesh):
    in_specs = (P("rad", None, "col", None), P("rad", "col", None), P(None, None, "rad"), P("rad"))
    out_specs = P("rad", None, "col", None)
    return jax.shard_map(
        on_device, mesh=mesh, in_specs=in_specs, out_specs=out_specs, check_vma=False
    )
```

```python
import jax
import jax.numpy as jnp
from jax import lax
from jax.experimental import pallas as pl
from jax.experimental.pallas import tpu as pltpu
from jax.sharding import PartitionSpec as P

SECTIONS = 2
CHUNKS = 4
PIECES = 4

diffusion_coeff = 0.2
advection_coeff = 0.15
rotation_coeff = 0.25

F32 = jnp.float32
BF16 = jnp.bfloat16
MB = 1 << 20


def shape(dims, dtype=F32):
    return jax.ShapeDtypeStruct(dims, dtype)


def cost(flops, moved):
    return pl.CostEstimate(flops=int(flops), bytes_accessed=int(moved), transcendentals=0)


def params(limit=40):
    return pltpu.CompilerParams(vmem_limit_bytes=limit * MB)


def stencil(cur, upper, lower, other, state):
    up = diffusion_coeff - advection_coeff * state
    down = diffusion_coeff + advection_coeff * state
    out = (1.0 - 2.0 * diffusion_coeff) * cur + up * upper + down * lower
    return out if other is None else out + other


def split(values):
    high = values.astype(BF16)
    return high, (values - high.astype(F32)).astype(BF16)


def product(x_parts, h_high, h_low):
    pairs = [split(x) for x in x_parts]
    high = jnp.concatenate([p[0] for p in pairs], axis=1)
    low = jnp.concatenate([p[1] for p in pairs], axis=1)

    def dot(a, b):
        return jnp.dot(a, b, preferred_element_type=F32)

    return dot(high, h_high) + (dot(high, h_low) + dot(low, h_high))


def state_kernel(where, state, rate, out, *, modes, nz):
    width = state.shape[1]
    for z in range(nz):
        out[z * width : (z + 1) * width, :] = state[pl.ds(z, modes, stride=nz), :].T
    if out.shape[0] > nz * width:
        out[nz * width :, :] = jnp.broadcast_to(rate[...], (out.shape[0] - nz * width, modes))


def turn_state(where, state, rate, foreign, extra):
    modes, nz, nphi = state.shape
    half = nphi // 2
    side = (lambda i, w: (0, 1 - (w[0] >> 1))) if foreign else (lambda i, w: (0, w[0] >> 1))
    rows = nz * half + extra
    return pl.pallas_call(
        lambda *refs: state_kernel(*refs, modes=modes, nz=nz),
        out_shape=shape((rows, modes)),
        grid_spec=pltpu.PrefetchScalarGridSpec(
            num_scalar_prefetch=1,
            grid=(1,),
            in_specs=[pl.BlockSpec((modes * nz, half), side), pl.BlockSpec((1, modes), lambda i, w: (0, 0))],
            out_specs=pl.BlockSpec((rows, modes), lambda i, w: (0, 0)),
        ),
        compiler_params=params(16),
        cost_estimate=cost(rows * modes, 8 * rows * modes),
        name="turn_state",
    )(where, state.reshape(modes * nz, nphi), rate)


def edge_kernel(where, cot, leading, last, *, modes, nz):
    for c in range(3):
        at = slice(c * modes, (c + 1) * modes)
        leading[at, :] = cot[pl.ds(c * nz, modes, stride=3 * nz), :]
        last[at, :] = cot[pl.ds(c * nz + nz - 1, modes, stride=3 * nz), :]


def edge_layers(where, cot, foreign):
    modes, comps, nz, nphi = cot.shape
    half = nphi // 2
    side = (lambda i, w: (0, 1 - (w[0] >> 1))) if foreign else (lambda i, w: (0, w[0] >> 1))
    return pl.pallas_call(
        lambda *refs: edge_kernel(*refs, modes=modes, nz=nz),
        out_shape=[shape((comps * modes, half))] * 2,
        grid_spec=pltpu.PrefetchScalarGridSpec(
            num_scalar_prefetch=1,
            grid=(1,),
            in_specs=[pl.BlockSpec((modes * comps * nz, half), side)],
            out_specs=[pl.BlockSpec((comps * modes, half), lambda i, w: (0, 0))] * 2,
        ),
        compiler_params=params(16),
        cost_estimate=cost(modes * comps * nphi, 4 * modes * comps * nz * half),
        name="edge_layers",
    )(where, cot.reshape(modes * comps * nz, nphi))


def blanks(*like):
    return pl.pallas_call(
        lambda *outs: None,
        out_shape=[shape(dims, dtype) for dims, dtype in like],
        out_specs=[pl.BlockSpec(memory_space=pl.ANY)] * len(like),
        name="blanks",
    )()


def first_kernel(where, cot, state, after, before, rate, *rest, modes, nz, chunks):
    outs, turned = rest[:-1], rest[-1]
    half = cot.shape[1]
    width = half // chunks
    for c in range(3):
        turned[c, 0] = before[c * modes : (c + 1) * modes, :].T
        for z in range(nz):
            turned[c, z + 1] = cot[pl.ds(c * nz + z, modes, stride=3 * nz), :].T
        turned[c, nz + 1] = after[c * modes : (c + 1) * modes, :].T
    turn = rotation_coeff * rate[...]
    for z in range(nz):
        for k in range(chunks):
            at = slice(k * width, (k + 1) * width)
            st = state[z * half + k * width : z * half + (k + 1) * width, :]
            cur = [turned[c, z + 1, at, :] for c in range(3)]
            others = (turn * cur[1], -turn * cur[0], None)
            for c in range(3):
                outs[k][c, z] = stencil(cur[c], turned[c, z + 2, at, :], turned[c, z, at, :], others[c], st)


def first_stencil(where, cot, state_turned, after, before, rate, foreign, chunks):
    modes, comps, nz, nphi = cot.shape
    half = nphi // 2
    side = (lambda i, w: (0, 1 - (w[0] >> 1))) if foreign else (lambda i, w: (0, w[0] >> 1))
    whole = lambda i, w: (0, 0)
    out = (comps, nz, half // chunks, modes)
    return pl.pallas_call(
        lambda *refs: first_kernel(*refs, modes=modes, nz=nz, chunks=chunks),
        out_shape=[shape(out)] * chunks,
        grid_spec=pltpu.PrefetchScalarGridSpec(
            num_scalar_prefetch=1,
            grid=(1,),
            in_specs=[
                pl.BlockSpec((modes * comps * nz, half), side),
                pl.BlockSpec((nz * half, modes), whole),
                pl.BlockSpec((comps * modes, half), whole),
                pl.BlockSpec((comps * modes, half), whole),
                pl.BlockSpec((1, modes), whole),
            ],
            out_specs=[pl.BlockSpec(out, lambda i, w: (0, 0, 0, 0))] * chunks,
            scratch_shapes=[pltpu.VMEM((comps, nz + 2, half, modes), F32)],
        ),
        compiler_params=params(32),
        cost_estimate=cost(12 * modes * comps * nz * half, 8 * modes * comps * nz * half),
        name="first_stencil",
    )(where, cot.reshape(modes * comps * nz, nphi), state_turned, after, before, rate)


def helm_kernel(where, own, far, high, low):
    for g, part in enumerate((own[...], far[0])):
        h, l = split(part)
        cols = slice(g * part.shape[2], (g + 1) * part.shape[2])
        high[:, :, cols] = h
        low[:, :, cols] = l


def split_helm(where, own, far):
    comps, rows, modes = own.shape
    block = lambda k, w: w[0] ^ (((k & 1) << 1) | (k >> 1))
    out = (comps, rows, 2 * modes)
    return pl.pallas_call(
        helm_kernel,
        out_shape=[shape(out, BF16)] * 2,
        grid_spec=pltpu.PrefetchScalarGridSpec(
            num_scalar_prefetch=1,
            grid=(rows // modes,),
            in_specs=[
                pl.BlockSpec((comps, modes, modes), lambda k, w: (0, block(k, w), 0)),
                pl.BlockSpec((1, comps, modes, modes), lambda k, w: (block(k, w) ^ w[1], 0, 0, 0)),
            ],
            out_specs=[pl.BlockSpec((comps, modes, 2 * modes), lambda k, w: (0, k, 0))] * 2,
        ),
        compiler_params=params(16),
        cost_estimate=cost(4 * comps * rows * modes, 16 * comps * rows * modes),
        name="split_helm",
    )(where, own, far)


def map1_kernel(own, far, own_peer, far_peer, high, low, out, first, last):
    _, nz, width, modes = own.shape
    rows = nz * width
    parts = [ref[0].reshape(rows, modes) for ref in (own, far, own_peer, far_peer)]
    res = product(parts, high[0], low[0]).reshape(nz, width, high.shape[2])
    out[0] = res
    first[0] = res[0]
    last[0] = res[nz - 1]


def map1(own, far, own_peer, far_peer, high, low, k):
    comps, nz, width, modes = far.shape
    rows, cols = high.shape[1:]
    here = pl.BlockSpec((1, nz, width, modes), lambda c: (c, 0, k, 0))
    chunk = pl.BlockSpec((1, nz, width, modes), lambda c: (c, 0, 0, 0))
    helm = pl.BlockSpec((1, rows, cols), lambda c: (c, 0, 0))
    layer = pl.BlockSpec((1, width, cols), lambda c: (c, 0, 0))
    return pl.pallas_call(
        map1_kernel,
        out_shape=[shape((comps, nz, width, cols)), shape((comps, width, cols)), shape((comps, width, cols))],
        grid=(comps,),
        in_specs=[here, chunk, here, chunk, helm, helm],
        out_specs=[pl.BlockSpec((1, nz, width, cols), lambda c: (c, 0, 0, 0)), layer, layer],
        compiler_params=params(24),
        cost_estimate=cost(6 * comps * nz * width * rows * cols, 4 * comps * (nz * width * (rows + cols) + rows * cols)),
        name=f"map1_{k}",
    )(own, far, own_peer, far_peer, high, low)


def second_kernel(cur, after, before, state_own, state_far, rate, out, *, k, half):
    comps, nz, width, cols = cur.shape
    modes = cols // 2
    rates = (rate[...], state_far[nz * half : nz * half + 1, :])
    for g in range(2):
        lanes = slice(g * modes, (g + 1) * modes)
        turn = rotation_coeff * rates[g]
        state = (state_own, state_far)[g]
        for z in range(nz):
            st = state[z * half + k * width : z * half + (k + 1) * width, :]
            here = [cur[c, z, :, lanes] for c in range(comps)]
            others = (turn * here[1], -turn * here[0], None)
            for c in range(comps):
                upper = cur[c, z + 1, :, lanes] if z + 1 < nz else after[c, :, lanes]
                lower = cur[c, z - 1, :, lanes] if z else before[c, :, lanes]
                out[c, z, :, lanes] = stencil(here[c], upper, lower, others[c], st)


def second_stencil(cur, after, before, state_own, state_far, rate, k, half):
    return pl.pallas_call(
        lambda *refs: second_kernel(*refs, k=k, half=half),
        out_shape=shape(cur.shape),
        compiler_params=params(16),
        cost_estimate=cost(12 * cur.size, 8 * cur.size),
        name=f"second_stencil_{k}",
    )(cur, after, before, state_own, state_far, rate)


def map2_kernel(own, peer, high, low, out_own, out_far):
    _, nz, width, cols = own.shape
    parts = [ref[0].reshape(nz * width, cols) for ref in (own, peer)]
    res = product(parts, high[0], low[0]).reshape(nz, width, cols)
    out_own[0] = res[:, :, : cols // 2]
    out_far[0] = res[:, :, cols // 2 :]


def map2(own, peer, high, low, k):
    comps, nz, width, cols = own.shape
    rows = high.shape[1]
    chunk = pl.BlockSpec((1, nz, width, cols), lambda c: (c, 0, 0, 0))
    helm = pl.BlockSpec((1, rows, cols), lambda c: (c, 0, 0))
    out = (comps, nz, width, cols // 2)
    return pl.pallas_call(
        map2_kernel,
        out_shape=[shape(out)] * 2,
        grid=(comps,),
        in_specs=[chunk, chunk, helm, helm],
        out_specs=[pl.BlockSpec((1, nz, width, cols // 2), lambda c: (c, 0, 0, 0))] * 2,
        compiler_params=params(24),
        cost_estimate=cost(6 * comps * nz * width * rows * cols, 4 * comps * (nz * width * (rows + cols) + rows * cols)),
        name=f"map2_{k}",
    )(own, peer, high, low)


def last_kernel(where, *refs, nz, chunks):
    ins, out = refs[:chunks], refs[-1]
    for z in range(nz):
        whole = jnp.concatenate([ref[0, z] for ref in ins], axis=0)
        out[:, z, :] = whole.T


def write_half(where, pieces, nphi, foreign, base=None):
    comps, nz, width, modes = pieces[0].shape
    chunks = len(pieces)
    side = (lambda c, w: (0, c, 1 - (w[0] >> 1))) if foreign else (lambda c, w: (0, c, w[0] >> 1))
    extra = () if base is None else (base,)
    return pl.pallas_call(
        lambda *refs: last_kernel(*refs, nz=nz, chunks=chunks),
        out_shape=shape((modes, comps * nz, nphi)),
        grid_spec=pltpu.PrefetchScalarGridSpec(
            num_scalar_prefetch=1,
            grid=(comps,),
            in_specs=[pl.BlockSpec((1,) + p.shape[1:], lambda c, w: (c, 0, 0, 0)) for p in pieces]
            + [pl.BlockSpec(memory_space=pl.ANY)] * len(extra),
            out_specs=pl.BlockSpec((modes, nz, nphi // 2), side),
        ),
        input_output_aliases={1 + chunks: 0} if extra else {},
        compiler_params=params(24),
        cost_estimate=cost(comps * nz * modes * nphi, 4 * comps * nz * modes * nphi),
        name="write_foreign" if foreign else "write_own",
    )(where, *pieces, *extra)


def tied(value, *others):
    return lax.optimization_barrier((value, *others))[0]


def on_device(cotangent, state_axial, helm_inverse, rotation_rate):
    modes, comps, nz, nphi = cotangent.shape
    half = nphi // 2
    peers, cols = lax.axis_size("rad"), lax.axis_size("col")
    up = [(i, (i + 1) % cols) for i in range(cols)]
    down = [(j, i) for i, j in up]

    def across(array):
        return lax.ppermute(array, "rad", [(i, i ^ 2) for i in range(peers)])

    def beside(array):
        return lax.ppermute(array, "rad", [(i, i ^ 1) for i in range(peers)])

    def hop(array, mask):
        return lax.ppermute(array, "col", [(i, i ^ mask) for i in range(cols)])

    lot = lax.axis_index("col").astype(jnp.int32) & (PIECES - 1)
    where = jnp.stack([lax.axis_index("rad").astype(jnp.int32), lot])
    rate = rotation_rate.reshape(1, modes)

    once = 1 + (where[0] >> 8)

    piece = across(lax.dynamic_slice_in_dim(helm_inverse, lot * modes, modes, axis=1))
    state_foreign = turn_state(where, state_axial, rate, True, 8)
    state_far = across(state_foreign)

    def halos(leading, last):
        return lax.ppermute(leading, "col", down), lax.ppermute(last, "col", up)

    def foreign_half(step, sent):
        here = where + (step >> 8)
        edges = halos(*edge_layers(here, cotangent, True))
        return tuple(first_stencil(here, cotangent, state_foreign, *edges, rate, True, CHUNKS))

    chunk = (comps, nz, half // CHUNKS, modes)
    sent = lax.fori_loop(0, once, foreign_half, tuple(blanks(*[(chunk, F32)] * CHUNKS)))
    far = [across(s) for k, s in enumerate(sent)]

    def own_half(step, carry):
        here = where + (step >> 8)
        edges = halos(*edge_layers(here, entry, False))
        helm_far, mask = tied(piece, here)[None], 1
        while mask < PIECES:
            helm_far = jnp.concatenate([helm_far, hop(helm_far, mask)])
            mask *= 2
        state_own = turn_state(here, state_axial, rate, False, 0)
        (own,) = first_stencil(here, entry, state_own, *edges, rate, False, 1)
        own_peer = beside(own)
        return (state_own, own, own_peer, *split_helm(here, helm_inverse, helm_far))

    entry = tied(cotangent, sent[0])
    columns = (comps, nz, half, modes)
    helm = (comps, peers * modes, 2 * modes)
    state_own, own, own_peer, high, low = lax.fori_loop(
        0, once, own_half, tuple(blanks(((nz * half, modes), F32), (columns, F32), (columns, F32), (helm, BF16), (helm, BF16)))
    )

    kept, back = [], []
    for k in range(CHUNKS):

        def chain(_, pair, k=k):
            here = pair[0]
            cur, leading, last = map1(own, here, own_peer, beside(here), high, low, k)
            nxt = second_stencil(cur, *halos(leading, last), state_own, state_far, rate, k, half)
            mine, theirs = map2(nxt, beside(nxt), high, low, k)
            return theirs, mine

        spare = tied(sent[k], kept[-1], back[0]) if k > 2 else tied(sent[k], kept[-1]) if k else sent[k]
        theirs, mine = lax.fori_loop(0, once, chain, (far[k], spare))
        kept.append(mine)
        back.append(across(theirs))
    out = write_half(where, kept, nphi, False)
    out = write_half(where, back, nphi, True, out)
    return out.reshape(modes, comps, nz, nphi)


def solution(mesh):
    in_specs = (P("rad", None, "col", None), P("rad", "col", None), P(None, None, "rad"), P("rad"))
    out_specs = P("rad", None, "col", None)
    return jax.shard_map(
        on_device, mesh=mesh, in_specs=in_specs, out_specs=out_specs, check_vma=False
    )
```

```python
import jax
import jax.numpy as jnp
from jax import lax
from jax.experimental import pallas as pl
from jax.experimental.pallas import tpu as pltpu
from jax.sharding import PartitionSpec as P

SECTIONS = 2
CHUNKS = 4
TOGETHER = 2
PIECES = 4

diffusion_coeff = 0.2
advection_coeff = 0.15
rotation_coeff = 0.25

F32 = jnp.float32
BF16 = jnp.bfloat16
MB = 1 << 20


def shape(dims, dtype=F32):
    return jax.ShapeDtypeStruct(dims, dtype)


def cost(flops, moved):
    return pl.CostEstimate(flops=int(flops), bytes_accessed=int(moved), transcendentals=0)


def params(limit=40):
    return pltpu.CompilerParams(vmem_limit_bytes=limit * MB)


def stencil(cur, upper, lower, other, state):
    up = diffusion_coeff - advection_coeff * state
    down = diffusion_coeff + advection_coeff * state
    out = (1.0 - 2.0 * diffusion_coeff) * cur + up * upper + down * lower
    return out if other is None else out + other


def split(values):
    high = values.astype(BF16)
    return high, (values - high.astype(F32)).astype(BF16)


def product(x_parts, h_high, h_low):
    pairs = [split(x) for x in x_parts]
    high = jnp.concatenate([p[0] for p in pairs], axis=1)
    low = jnp.concatenate([p[1] for p in pairs], axis=1)

    def dot(a, b):
        return jnp.dot(a, b, preferred_element_type=F32)

    return dot(high, h_high) + (dot(high, h_low) + dot(low, h_high))


def state_kernel(where, state, rate, out, *, modes, nz):
    width = state.shape[1]
    for z in range(nz):
        out[z * width : (z + 1) * width, :] = state[pl.ds(z, modes, stride=nz), :].T
    if out.shape[0] > nz * width:
        out[nz * width :, :] = jnp.broadcast_to(rate[...], (out.shape[0] - nz * width, modes))


def turn_state(where, state, rate, foreign, extra):
    modes, nz, nphi = state.shape
    half = nphi // 2
    side = (lambda i, w: (0, 1 - (w[0] >> 1))) if foreign else (lambda i, w: (0, w[0] >> 1))
    rows = nz * half + extra
    return pl.pallas_call(
        lambda *refs: state_kernel(*refs, modes=modes, nz=nz),
        out_shape=shape((rows, modes)),
        grid_spec=pltpu.PrefetchScalarGridSpec(
            num_scalar_prefetch=1,
            grid=(1,),
            in_specs=[pl.BlockSpec((modes * nz, half), side), pl.BlockSpec((1, modes), lambda i, w: (0, 0))],
            out_specs=pl.BlockSpec((rows, modes), lambda i, w: (0, 0)),
        ),
        compiler_params=params(16),
        cost_estimate=cost(rows * modes, 8 * rows * modes),
        name="turn_state",
    )(where, state.reshape(modes * nz, nphi), rate)


def edge_kernel(where, cot, leading, last, *, modes, nz):
    for c in range(3):
        at = slice(c * modes, (c + 1) * modes)
        leading[at, :] = cot[pl.ds(c * nz, modes, stride=3 * nz), :]
        last[at, :] = cot[pl.ds(c * nz + nz - 1, modes, stride=3 * nz), :]


def edge_layers(where, cot, foreign):
    modes, comps, nz, nphi = cot.shape
    half = nphi // 2
    side = (lambda i, w: (0, 1 - (w[0] >> 1))) if foreign else (lambda i, w: (0, w[0] >> 1))
    return pl.pallas_call(
        lambda *refs: edge_kernel(*refs, modes=modes, nz=nz),
        out_shape=[shape((comps * modes, half))] * 2,
        grid_spec=pltpu.PrefetchScalarGridSpec(
            num_scalar_prefetch=1,
            grid=(1,),
            in_specs=[pl.BlockSpec((modes * comps * nz, half), side)],
            out_specs=[pl.BlockSpec((comps * modes, half), lambda i, w: (0, 0))] * 2,
        ),
        compiler_params=params(16),
        cost_estimate=cost(modes * comps * nphi, 4 * modes * comps * nz * half),
        name="edge_layers",
    )(where, cot.reshape(modes * comps * nz, nphi))


def blanks(*like):
    return pl.pallas_call(
        lambda *outs: None,
        out_shape=[shape(dims, dtype) for dims, dtype in like],
        out_specs=[pl.BlockSpec(memory_space=pl.ANY)] * len(like),
        name="blanks",
    )()


def first_kernel(where, cot, state, after, before, rate, *rest, modes, nz, chunks):
    outs, turned = rest[:-1], rest[-1]
    half = cot.shape[1]
    width = half // chunks
    for c in range(3):
        turned[c, 0] = before[c * modes : (c + 1) * modes, :].T
        for z in range(nz):
            turned[c, z + 1] = cot[pl.ds(c * nz + z, modes, stride=3 * nz), :].T
        turned[c, nz + 1] = after[c * modes : (c + 1) * modes, :].T
    turn = rotation_coeff * rate[...]
    for z in range(nz):
        for k in range(chunks):
            at = slice(k * width, (k + 1) * width)
            st = state[z * half + k * width : z * half + (k + 1) * width, :]
            cur = [turned[c, z + 1, at, :] for c in range(3)]
            others = (turn * cur[1], -turn * cur[0], None)
            for c in range(3):
                outs[k][c, z] = stencil(cur[c], turned[c, z + 2, at, :], turned[c, z, at, :], others[c], st)


def first_stencil(where, cot, state_turned, after, before, rate, foreign, chunks):
    modes, comps, nz, nphi = cot.shape
    half = nphi // 2
    side = (lambda i, w: (0, 1 - (w[0] >> 1))) if foreign else (lambda i, w: (0, w[0] >> 1))
    whole = lambda i, w: (0, 0)
    out = (comps, nz, half // chunks, modes)
    return pl.pallas_call(
        lambda *refs: first_kernel(*refs, modes=modes, nz=nz, chunks=chunks),
        out_shape=[shape(out)] * chunks,
        grid_spec=pltpu.PrefetchScalarGridSpec(
            num_scalar_prefetch=1,
            grid=(1,),
            in_specs=[
                pl.BlockSpec((modes * comps * nz, half), side),
                pl.BlockSpec((nz * half, modes), whole),
                pl.BlockSpec((comps * modes, half), whole),
                pl.BlockSpec((comps * modes, half), whole),
                pl.BlockSpec((1, modes), whole),
            ],
            out_specs=[pl.BlockSpec(out, lambda i, w: (0, 0, 0, 0))] * chunks,
            scratch_shapes=[pltpu.VMEM((comps, nz + 2, half, modes), F32)],
        ),
        compiler_params=params(32),
        cost_estimate=cost(12 * modes * comps * nz * half, 8 * modes * comps * nz * half),
        name="first_stencil",
    )(where, cot.reshape(modes * comps * nz, nphi), state_turned, after, before, rate)


def helm_kernel(where, own, far, high, low):
    for g, part in enumerate((own[...], far[0])):
        h, l = split(part)
        cols = slice(g * part.shape[2], (g + 1) * part.shape[2])
        high[:, :, cols] = h
        low[:, :, cols] = l


def split_helm(where, own, far):
    comps, rows, modes = own.shape
    block = lambda k, w: w[0] ^ (((k & 1) << 1) | (k >> 1))
    out = (comps, rows, 2 * modes)
    return pl.pallas_call(
        helm_kernel,
        out_shape=[shape(out, BF16)] * 2,
        grid_spec=pltpu.PrefetchScalarGridSpec(
            num_scalar_prefetch=1,
            grid=(rows // modes,),
            in_specs=[
                pl.BlockSpec((comps, modes, modes), lambda k, w: (0, block(k, w), 0)),
                pl.BlockSpec((1, comps, modes, modes), lambda k, w: (block(k, w) ^ w[1], 0, 0, 0)),
            ],
            out_specs=[pl.BlockSpec((comps, modes, 2 * modes), lambda k, w: (0, k, 0))] * 2,
        ),
        compiler_params=params(16),
        cost_estimate=cost(4 * comps * rows * modes, 16 * comps * rows * modes),
        name="split_helm",
    )(where, own, far)


def map1_kernel(own, far, own_peer, far_peer, high, low, out, first, last):
    _, nz, width, modes = own.shape
    rows = nz * width
    parts = [ref[0].reshape(rows, modes) for ref in (own, far, own_peer, far_peer)]
    res = product(parts, high[0], low[0]).reshape(nz, width, high.shape[2])
    out[0] = res
    first[0] = res[0]
    last[0] = res[nz - 1]


def map1(own, far, own_peer, far_peer, high, low, k):
    comps, nz, width, modes = far.shape
    rows, cols = high.shape[1:]
    here = pl.BlockSpec((1, nz, width, modes), lambda c: (c, 0, k, 0))
    chunk = pl.BlockSpec((1, nz, width, modes), lambda c: (c, 0, 0, 0))
    helm = pl.BlockSpec((1, rows, cols), lambda c: (c, 0, 0))
    layer = pl.BlockSpec((1, width, cols), lambda c: (c, 0, 0))
    return pl.pallas_call(
        map1_kernel,
        out_shape=[shape((comps, nz, width, cols)), shape((comps, width, cols)), shape((comps, width, cols))],
        grid=(comps,),
        in_specs=[here, chunk, here, chunk, helm, helm],
        out_specs=[pl.BlockSpec((1, nz, width, cols), lambda c: (c, 0, 0, 0)), layer, layer],
        compiler_params=params(24),
        cost_estimate=cost(6 * comps * nz * width * rows * cols, 4 * comps * (nz * width * (rows + cols) + rows * cols)),
        name=f"map1_{k}",
    )(own, far, own_peer, far_peer, high, low)


def second_kernel(cur, after, before, state_own, state_far, rate, out, *, k, half):
    comps, nz, width, cols = cur.shape
    modes = cols // 2
    rates = (rate[...], state_far[nz * half : nz * half + 1, :])
    for g in range(2):
        lanes = slice(g * modes, (g + 1) * modes)
        turn = rotation_coeff * rates[g]
        state = (state_own, state_far)[g]
        for z in range(nz):
            st = state[z * half + k * width : z * half + (k + 1) * width, :]
            here = [cur[c, z, :, lanes] for c in range(comps)]
            others = (turn * here[1], -turn * here[0], None)
            for c in range(comps):
                upper = cur[c, z + 1, :, lanes] if z + 1 < nz else after[c, :, lanes]
                lower = cur[c, z - 1, :, lanes] if z else before[c, :, lanes]
                out[c, z, :, lanes] = stencil(here[c], upper, lower, others[c], st)


def second_stencil(cur, after, before, state_own, state_far, rate, k, half):
    return pl.pallas_call(
        lambda *refs: second_kernel(*refs, k=k, half=half),
        out_shape=shape(cur.shape),
        compiler_params=params(16),
        cost_estimate=cost(12 * cur.size, 8 * cur.size),
        name=f"second_stencil_{k}",
    )(cur, after, before, state_own, state_far, rate)


def map2_kernel(own, peer, high, low, out_own, out_far):
    _, nz, width, cols = own.shape
    parts = [ref[0].reshape(nz * width, cols) for ref in (own, peer)]
    res = product(parts, high[0], low[0]).reshape(nz, width, cols)
    out_own[0] = res[:, :, : cols // 2]
    out_far[0] = res[:, :, cols // 2 :]


def map2(own, peer, high, low, k):
    comps, nz, width, cols = own.shape
    rows = high.shape[1]
    chunk = pl.BlockSpec((1, nz, width, cols), lambda c: (c, 0, 0, 0))
    helm = pl.BlockSpec((1, rows, cols), lambda c: (c, 0, 0))
    out = (comps, nz, width, cols // 2)
    return pl.pallas_call(
        map2_kernel,
        out_shape=[shape(out)] * 2,
        grid=(comps,),
        in_specs=[chunk, chunk, helm, helm],
        out_specs=[pl.BlockSpec((1, nz, width, cols // 2), lambda c: (c, 0, 0, 0))] * 2,
        compiler_params=params(24),
        cost_estimate=cost(6 * comps * nz * width * rows * cols, 4 * comps * (nz * width * (rows + cols) + rows * cols)),
        name=f"map2_{k}",
    )(own, peer, high, low)


def last_kernel(where, *refs, nz, chunks):
    ins, out = refs[:chunks], refs[-1]
    for z in range(nz):
        whole = jnp.concatenate([ref[0, z] for ref in ins], axis=0)
        out[:, z, :] = whole.T


def write_half(where, pieces, nphi, foreign, base=None):
    comps, nz, width, modes = pieces[0].shape
    chunks = len(pieces)
    side = (lambda c, w: (0, c, 1 - (w[0] >> 1))) if foreign else (lambda c, w: (0, c, w[0] >> 1))
    extra = () if base is None else (base,)
    return pl.pallas_call(
        lambda *refs: last_kernel(*refs, nz=nz, chunks=chunks),
        out_shape=shape((modes, comps * nz, nphi)),
        grid_spec=pltpu.PrefetchScalarGridSpec(
            num_scalar_prefetch=1,
            grid=(comps,),
            in_specs=[pl.BlockSpec((1,) + p.shape[1:], lambda c, w: (c, 0, 0, 0)) for p in pieces]
            + [pl.BlockSpec(memory_space=pl.ANY)] * len(extra),
            out_specs=pl.BlockSpec((modes, nz, nphi // 2), side),
        ),
        input_output_aliases={1 + chunks: 0} if extra else {},
        compiler_params=params(24),
        cost_estimate=cost(comps * nz * modes * nphi, 4 * comps * nz * modes * nphi),
        name="write_foreign" if foreign else "write_own",
    )(where, *pieces, *extra)


def tied(value, *others):
    return lax.optimization_barrier((value, *others))[0]


def on_device(cotangent, state_axial, helm_inverse, rotation_rate):
    modes, comps, nz, nphi = cotangent.shape
    half = nphi // 2
    peers, cols = lax.axis_size("rad"), lax.axis_size("col")
    up = [(i, (i + 1) % cols) for i in range(cols)]
    down = [(j, i) for i, j in up]

    def across(array):
        return lax.ppermute(array, "rad", [(i, i ^ 2) for i in range(peers)])

    def beside(array):
        return lax.ppermute(array, "rad", [(i, i ^ 1) for i in range(peers)])

    def hop(array, mask):
        return lax.ppermute(array, "col", [(i, i ^ mask) for i in range(cols)])

    lot = lax.axis_index("col").astype(jnp.int32) & (PIECES - 1)
    where = jnp.stack([lax.axis_index("rad").astype(jnp.int32), lot])
    rate = rotation_rate.reshape(1, modes)

    once = 1 + (where[0] >> 8)

    piece = across(lax.dynamic_slice_in_dim(helm_inverse, lot * modes, modes, axis=1))
    state_foreign = turn_state(where, state_axial, rate, True, 8)
    state_far = across(state_foreign)

    def halos(leading, last):
        return lax.ppermute(leading, "col", down), lax.ppermute(last, "col", up)

    def foreign_half(step, sent):
        here = where + (step >> 8)
        edges = halos(*edge_layers(here, cotangent, True))
        return tuple(first_stencil(here, cotangent, state_foreign, *edges, rate, True, CHUNKS))

    chunk = (comps, nz, half // CHUNKS, modes)
    sent = lax.fori_loop(0, once, foreign_half, tuple(blanks(*[(chunk, F32)] * CHUNKS)))
    far = [across(tied(s, state_far) if k >= TOGETHER else s) for k, s in enumerate(sent)]

    def own_half(step, carry):
        here = where + (step >> 8)
        edges = halos(*edge_layers(here, entry, False))
        helm_far, mask = tied(piece, here)[None], 1
        while mask < PIECES:
            helm_far = jnp.concatenate([helm_far, hop(helm_far, mask)])
            if mask == 1:
                edges = tuple(tied(e, helm_far) for e in edges)
            mask *= 2
        state_own = turn_state(here, state_axial, rate, False, 0)
        (own,) = first_stencil(here, entry, state_own, *edges, rate, False, 1)
        own_peer = beside(own)
        return (state_own, own, own_peer, *split_helm(here, helm_inverse, helm_far))

    entry = tied(cotangent, sent[0])
    columns = (comps, nz, half, modes)
    helm = (comps, peers * modes, 2 * modes)
    state_own, own, own_peer, high, low = lax.fori_loop(
        0, once, own_half, tuple(blanks(((nz * half, modes), F32), (columns, F32), (columns, F32), (helm, BF16), (helm, BF16)))
    )

    kept, back = [], []
    for first in range(0, CHUNKS, TOGETHER):
        group = range(first, first + TOGETHER)

        def chains(_, carry, group=group):
            here = carry[:TOGETHER]
            there = [beside(h) for h in here]
            moved = []
            for k, h, t in zip(group, here, there):
                cur, leading, last = map1(own, h, own_peer, t, high, low, k)
                moved.append((cur, *halos(leading, last)))
            nxt = [second_stencil(*m, state_own, state_far, rate, k, half) for k, m in zip(group, moved)]
            there = [beside(n) for n in nxt]
            results = [map2(n, t, high, low, k) for k, n, t in zip(group, nxt, there)]
            return tuple(r[1] for r in results) + tuple(r[0] for r in results)

        spare = [tied(sent[k], kept[-1]) if kept else sent[k] for k in group]
        results = lax.fori_loop(0, once, chains, (*[far[k] for k in group], *spare))
        kept += results[TOGETHER:]
        back += [across(t) for t in results[:TOGETHER]]
    out = write_half(where, kept, nphi, False)
    out = write_half(where, back, nphi, True, out)
    return out.reshape(modes, comps, nz, nphi)


def solution(mesh):
    in_specs = (P("rad", None, "col", None), P("rad", "col", None), P(None, None, "rad"), P("rad"))
    out_specs = P("rad", None, "col", None)
    return jax.shard_map(
        on_device, mesh=mesh, in_specs=in_specs, out_specs=out_specs, check_vma=False
    )
```

```python
import jax
import jax.numpy as jnp
from jax import lax
from jax.experimental import pallas as pl
from jax.experimental.pallas import tpu as pltpu
from jax.sharding import PartitionSpec as P

SECTIONS = 2
GROUPS = 2
PARTS = 2
RATE_ROWS = 8
PIECES = 4

diffusion_coeff = 0.2
advection_coeff = 0.15
rotation_coeff = 0.25

F32 = jnp.float32
BF16 = jnp.bfloat16
MB = 1 << 20


def shape(dims, dtype=F32):
    return jax.ShapeDtypeStruct(dims, dtype)


def cost(flops, moved):
    return pl.CostEstimate(flops=int(flops), bytes_accessed=int(moved), transcendentals=0)


def params(limit=40):
    return pltpu.CompilerParams(vmem_limit_bytes=limit * MB)


def stencil(cur, upper, lower, other, state):
    up = diffusion_coeff - advection_coeff * state
    down = diffusion_coeff + advection_coeff * state
    out = (1.0 - 2.0 * diffusion_coeff) * cur + up * upper + down * lower
    return out if other is None else out + other


def split(values):
    high = values.astype(BF16)
    return high, (values - high.astype(F32)).astype(BF16)


def product(x_parts, h_high, h_low):
    pairs = [split(x) for x in x_parts]
    high = jnp.concatenate([p[0] for p in pairs], axis=1)
    low = jnp.concatenate([p[1] for p in pairs], axis=1)

    def dot(a, b):
        return jnp.dot(a, b, preferred_element_type=F32)

    return dot(high, h_high) + (dot(high, h_low) + dot(low, h_high))


def state_kernel(where, state, *refs, modes, nz):
    out = refs[-1]
    width = state.shape[1]
    rows = nz * width
    for z in range(nz):
        out[z * width : (z + 1) * width, :] = state[pl.ds(z, modes, stride=nz), :].T
    if len(refs) > 1:
        rate, helm = refs[:2]
        out[rows : rows + RATE_ROWS, :] = jnp.broadcast_to(rate[...], (RATE_ROWS, modes))
        out[rows + RATE_ROWS :, :] = helm[...].reshape(-1, modes)


def turn_state(where, state, foreign, rate=None, helm=None):
    modes, nz, nphi = state.shape
    half = nphi // 2
    side = (lambda i, w: (0, 1 - (w[0] >> 1))) if foreign else (lambda i, w: (0, w[0] >> 1))
    rows, more, more_specs = nz * half, (), []
    if helm is not None:
        comps = helm.shape[0]
        rows += RATE_ROWS + comps * modes
        more = (rate, helm)
        more_specs = [
            pl.BlockSpec((1, modes), lambda i, w: (0, 0)),
            pl.BlockSpec((comps, modes, modes), lambda i, w: (0, w[1], 0)),
        ]
    return pl.pallas_call(
        lambda *refs: state_kernel(*refs, modes=modes, nz=nz),
        out_shape=shape((rows, modes)),
        grid_spec=pltpu.PrefetchScalarGridSpec(
            num_scalar_prefetch=1,
            grid=(1,),
            in_specs=[pl.BlockSpec((modes * nz, half), side)] + more_specs,
            out_specs=pl.BlockSpec((rows, modes), lambda i, w: (0, 0)),
        ),
        compiler_params=params(16),
        cost_estimate=cost(rows * modes, 8 * rows * modes),
        name="turn_state",
    )(where, state.reshape(modes * nz, nphi), *more)


def edge_kernel(where, cot, leading, last, *, modes, nz):
    for c in range(3):
        at = slice(c * modes, (c + 1) * modes)
        leading[at, :] = cot[pl.ds(c * nz, modes, stride=3 * nz), :]
        last[at, :] = cot[pl.ds(c * nz + nz - 1, modes, stride=3 * nz), :]


def edge_layers(where, cot, foreign):
    modes, comps, nz, nphi = cot.shape
    half = nphi // 2
    side = (lambda i, w: (0, 1 - (w[0] >> 1))) if foreign else (lambda i, w: (0, w[0] >> 1))
    return pl.pallas_call(
        lambda *refs: edge_kernel(*refs, modes=modes, nz=nz),
        out_shape=[shape((comps * modes, half))] * 2,
        grid_spec=pltpu.PrefetchScalarGridSpec(
            num_scalar_prefetch=1,
            grid=(1,),
            in_specs=[pl.BlockSpec((modes * comps * nz, half), side)],
            out_specs=[pl.BlockSpec((comps * modes, half), lambda i, w: (0, 0))] * 2,
        ),
        compiler_params=params(16),
        cost_estimate=cost(modes * comps * nphi, 4 * modes * comps * nz * half),
        name="edge_layers",
    )(where, cot.reshape(modes * comps * nz, nphi))


def blanks(*like):
    return pl.pallas_call(
        lambda *outs: None,
        out_shape=[shape(dims, dtype) for dims, dtype in like],
        out_specs=[pl.BlockSpec(memory_space=pl.ANY)] * len(like),
        name="blanks",
    )()


def first_kernel(where, cot, state, after, before, rate, *rest, modes, nz, chunks):
    outs, turned = rest[:-1], rest[-1]
    half = cot.shape[1]
    width = half // chunks
    for c in range(3):
        turned[c, 0] = before[c * modes : (c + 1) * modes, :].T
        for z in range(nz):
            turned[c, z + 1] = cot[pl.ds(c * nz + z, modes, stride=3 * nz), :].T
        turned[c, nz + 1] = after[c * modes : (c + 1) * modes, :].T
    turn = rotation_coeff * rate[...]
    for z in range(nz):
        for k in range(chunks):
            at = slice(k * width, (k + 1) * width)
            st = state[z * half + k * width : z * half + (k + 1) * width, :]
            cur = [turned[c, z + 1, at, :] for c in range(3)]
            others = (turn * cur[1], -turn * cur[0], None)
            for c in range(3):
                outs[k][c, z] = stencil(cur[c], turned[c, z + 2, at, :], turned[c, z, at, :], others[c], st)


def first_stencil(where, cot, state_turned, after, before, rate, foreign, chunks):
    modes, comps, nz, nphi = cot.shape
    half = nphi // 2
    side = (lambda i, w: (0, 1 - (w[0] >> 1))) if foreign else (lambda i, w: (0, w[0] >> 1))
    whole = lambda i, w: (0, 0)
    out = (comps, nz, half // chunks, modes)
    return pl.pallas_call(
        lambda *refs: first_kernel(*refs, modes=modes, nz=nz, chunks=chunks),
        out_shape=[shape(out)] * chunks,
        grid_spec=pltpu.PrefetchScalarGridSpec(
            num_scalar_prefetch=1,
            grid=(1,),
            in_specs=[
                pl.BlockSpec((modes * comps * nz, half), side),
                pl.BlockSpec((nz * half, modes), whole),
                pl.BlockSpec((comps * modes, half), whole),
                pl.BlockSpec((comps * modes, half), whole),
                pl.BlockSpec((1, modes), whole),
            ],
            out_specs=[pl.BlockSpec(out, lambda i, w: (0, 0, 0, 0))] * chunks,
            scratch_shapes=[pltpu.VMEM((comps, nz + 2, half, modes), F32)],
        ),
        compiler_params=params(32),
        cost_estimate=cost(12 * modes * comps * nz * half, 8 * modes * comps * nz * half),
        name="first_stencil",
    )(where, cot.reshape(modes * comps * nz, nphi), state_turned, after, before, rate)


def helm_kernel(where, own, *refs):
    far, (high, low) = refs[:-2], refs[-2:]
    rows, modes = own.shape[1:]
    k = pl.program_id(0)
    wanted = block_of(k, where) ^ where[1]
    h, l = split(own[...])
    high[:, :, :modes] = h
    low[:, :, :modes] = l
    for d, ref in enumerate(far):

        @pl.when(wanted == d)
        def _(ref=ref):
            h, l = split(ref[...])
            high[:, :, modes:] = h
            low[:, :, modes:] = l


def block_of(k, where):
    return where[0] ^ (((k & 1) << 1) | (k >> 1))


def split_helm(where, own, far):
    comps, rows, modes = own.shape
    out = (comps, rows, 2 * modes)
    return pl.pallas_call(
        helm_kernel,
        out_shape=[shape(out, BF16)] * 2,
        grid_spec=pltpu.PrefetchScalarGridSpec(
            num_scalar_prefetch=1,
            grid=(rows // modes,),
            in_specs=[pl.BlockSpec((comps, modes, modes), lambda k, w: (0, block_of(k, w), 0))]
            + [pl.BlockSpec((comps, modes, modes), lambda k, w: (0, 0, 0))] * len(far),
            out_specs=[pl.BlockSpec((comps, modes, 2 * modes), lambda k, w: (0, k, 0))] * 2,
        ),
        compiler_params=params(16),
        cost_estimate=cost(4 * comps * rows * modes, 16 * comps * rows * modes),
        name="split_helm",
    )(where, own, *far)


def map1_kernel(own, far, own_peer, far_peer, high, low, out, first, last):
    _, nz, width, modes = own.shape
    rows = nz * width
    parts = [ref[0].reshape(rows, modes) for ref in (own, far, own_peer, far_peer)]
    res = product(parts, high[0], low[0]).reshape(nz, width, high.shape[2])
    out[0] = res
    first[0] = res[0]
    last[0] = res[nz - 1]


def map1(own, far, own_peer, far_peer, high, low, k):
    comps, nz, width, modes = far.shape
    width //= PARTS
    rows, cols = high.shape[1:]
    here = pl.BlockSpec((1, nz, width, modes), lambda c: (c, 0, k, 0))
    chunk = pl.BlockSpec((1, nz, width, modes), lambda c: (c, 0, k % PARTS, 0))
    helm = pl.BlockSpec((1, rows, cols), lambda c: (c, 0, 0))
    layer = pl.BlockSpec((1, width, cols), lambda c: (c, 0, 0))
    return pl.pallas_call(
        map1_kernel,
        out_shape=[shape((comps, nz, width, cols)), shape((comps, width, cols)), shape((comps, width, cols))],
        grid=(comps,),
        in_specs=[here, chunk, here, chunk, helm, helm],
        out_specs=[pl.BlockSpec((1, nz, width, cols), lambda c: (c, 0, 0, 0)), layer, layer],
        compiler_params=params(24),
        cost_estimate=cost(6 * comps * nz * width * rows * cols, 4 * comps * (nz * width * (rows + cols) + rows * cols)),
        name=f"map1_{k}",
    )(own, far, own_peer, far_peer, high, low)


def second_kernel(cur, after, before, state_own, state_far, rate, out, *, k, half):
    comps, nz, width, cols = cur.shape
    modes = cols // 2
    rates = (rate[...], state_far[nz * half : nz * half + 1, :])
    for g in range(2):
        lanes = slice(g * modes, (g + 1) * modes)
        turn = rotation_coeff * rates[g]
        state = (state_own, state_far)[g]
        for z in range(nz):
            st = state[z * half + k * width : z * half + (k + 1) * width, :]
            here = [cur[c, z, :, lanes] for c in range(comps)]
            others = (turn * here[1], -turn * here[0], None)
            for c in range(comps):
                upper = cur[c, z + 1, :, lanes] if z + 1 < nz else after[c, :, lanes]
                lower = cur[c, z - 1, :, lanes] if z else before[c, :, lanes]
                out[c, z, :, lanes] = stencil(here[c], upper, lower, others[c], st)


def second_stencil(cur, after, before, state_own, state_far, rate, k, half):
    return pl.pallas_call(
        lambda *refs: second_kernel(*refs, k=k, half=half),
        out_shape=shape(cur.shape),
        compiler_params=params(16),
        cost_estimate=cost(12 * cur.size, 8 * cur.size),
        name=f"second_stencil_{k}",
    )(cur, after, before, state_own, state_far, rate)


def map2_kernel(own, peer, high, low, *refs):
    out_own, out_far = refs[-2:]
    _, nz, width, cols = own.shape
    parts = [ref[0].reshape(nz * width, cols) for ref in (own, peer)]
    res = product(parts, high[0], low[0]).reshape(nz, width, cols)
    out_own[0] = res[:, :, : cols // 2]
    out_far[0] = res[:, :, cols // 2 :]


def map2(own, peer, high, low, k, base):
    comps, nz, width, cols = own.shape
    rows = high.shape[1]
    chunk = pl.BlockSpec((1, nz, width, cols), lambda c: (c, 0, 0, 0))
    helm = pl.BlockSpec((1, rows, cols), lambda c: (c, 0, 0))
    out = (comps, nz, width * PARTS, cols // 2)
    return pl.pallas_call(
        map2_kernel,
        out_shape=[shape(out)] * 2,
        grid=(comps,),
        in_specs=[chunk, chunk, helm, helm] + [pl.BlockSpec(memory_space=pl.ANY)] * len(base),
        out_specs=[pl.BlockSpec((1, nz, width, cols // 2), lambda c: (c, 0, k % PARTS, 0))] * 2,
        input_output_aliases={4 + i: i for i in range(len(base))},
        compiler_params=params(24),
        cost_estimate=cost(6 * comps * nz * width * rows * cols, 4 * comps * (nz * width * (rows + cols) + rows * cols)),
        name=f"map2_{k}",
    )(own, peer, high, low, *base)


def last_kernel(where, *refs, nz, chunks):
    ins, out = refs[:chunks], refs[-1]
    for z in range(nz):
        whole = jnp.concatenate([ref[0, z] for ref in ins], axis=0)
        out[:, z, :] = whole.T


def write_half(where, pieces, nphi, foreign, base=None):
    comps, nz, width, modes = pieces[0].shape
    chunks = len(pieces)
    side = (lambda c, w: (0, c, 1 - (w[0] >> 1))) if foreign else (lambda c, w: (0, c, w[0] >> 1))
    extra = () if base is None else (base,)
    return pl.pallas_call(
        lambda *refs: last_kernel(*refs, nz=nz, chunks=chunks),
        out_shape=shape((modes, comps * nz, nphi)),
        grid_spec=pltpu.PrefetchScalarGridSpec(
            num_scalar_prefetch=1,
            grid=(comps,),
            in_specs=[pl.BlockSpec((1,) + p.shape[1:], lambda c, w: (c, 0, 0, 0)) for p in pieces]
            + [pl.BlockSpec(memory_space=pl.ANY)] * len(extra),
            out_specs=pl.BlockSpec((modes, nz, nphi // 2), side),
        ),
        input_output_aliases={1 + chunks: 0} if extra else {},
        compiler_params=params(24),
        cost_estimate=cost(comps * nz * modes * nphi, 4 * comps * nz * modes * nphi),
        name="write_foreign" if foreign else "write_own",
    )(where, *pieces, *extra)


def tied(value, *others):
    return lax.optimization_barrier((value, *others))[0]


def on_device(cotangent, state_axial, helm_inverse, rotation_rate):
    modes, comps, nz, nphi = cotangent.shape
    half = nphi // 2
    peers, cols = lax.axis_size("rad"), lax.axis_size("col")
    up = [(i, (i + 1) % cols) for i in range(cols)]
    down = [(j, i) for i, j in up]

    def across(array):
        return lax.ppermute(array, "rad", [(i, i ^ 2) for i in range(peers)])

    def beside(array):
        return lax.ppermute(array, "rad", [(i, i ^ 1) for i in range(peers)])

    def hop(array, mask):
        return lax.ppermute(array, "col", [(i, i ^ mask) for i in range(cols)])

    lot = lax.axis_index("col").astype(jnp.int32) & (PIECES - 1)
    where = jnp.stack([lax.axis_index("rad").astype(jnp.int32), lot])
    rate = rotation_rate.reshape(1, modes)

    once = 1 + (where[0] >> 8)

    state_foreign = turn_state(where, state_axial, True, rate, helm_inverse)
    state_far = across(state_foreign)

    def halos(leading, last):
        return lax.ppermute(leading, "col", down), lax.ppermute(last, "col", up)

    def foreign_half(step, sent):
        here = where + (step >> 8)
        edges = halos(*edge_layers(here, cotangent, True))
        return tuple(first_stencil(here, cotangent, state_foreign, *edges, rate, True, GROUPS))

    chunk = (comps, nz, half // GROUPS, modes)
    sent = lax.fori_loop(0, once, foreign_half, tuple(blanks(*[(chunk, F32)] * GROUPS)))
    far = [across(tied(s, state_far) if k else s) for k, s in enumerate(sent)]

    def own_half(step, carry):
        here = where + (step >> 8)
        edges = halos(*edge_layers(here, entry, False))
        blocks = [tied(state_far, here)[nz * half + RATE_ROWS :].reshape(comps, modes, modes)]
        blocks += [hop(blocks[0], 1), hop(blocks[0], 2)]
        blocks += [hop(blocks[2], 1)]
        edges = tuple(tied(e, *blocks[1:]) for e in edges)
        state_own = turn_state(here, state_axial, False)
        (own,) = first_stencil(here, entry, state_own, *edges, rate, False, 1)
        own_peer = beside(own)
        return (state_own, own, own_peer, *split_helm(here, helm_inverse, blocks))

    entry = tied(cotangent, sent[0], state_far)
    columns = (comps, nz, half, modes)
    helm = (comps, peers * modes, 2 * modes)
    state_own, own, own_peer, high, low = lax.fori_loop(
        0, once, own_half, tuple(blanks(((nz * half, modes), F32), (columns, F32), (columns, F32), (helm, BF16), (helm, BF16)))
    )

    kept, back = [], []
    for g in range(GROUPS):
        group = range(g * PARTS, (g + 1) * PARTS)

        def chains(_, carry, group=group):
            here = carry[0]
            there = beside(here)
            moved = []
            for k in group:
                cur, leading, last = map1(own, here, own_peer, there, high, low, k)
                moved.append((cur, *halos(leading, last)))
            moved = lax.optimization_barrier(tuple(moved))
            nxt = [second_stencil(*m, state_own, state_far, rate, k, half) for k, m in zip(group, moved)]
            there = [beside(n) for n in nxt]
            mine_theirs = ()
            for k, n, t in zip(group, nxt, there):
                mine_theirs = tuple(map2(n, t, high, low, k, mine_theirs))
            return mine_theirs[::-1]

        spare = tied(sent[g], kept[-1]) if kept else sent[g]
        theirs, mine = lax.fori_loop(0, once, chains, (far[g], spare))
        kept.append(mine)
        back.append(across(theirs))
    out = write_half(where, kept, nphi, False)
    out = write_half(where, back, nphi, True, out)
    return out.reshape(modes, comps, nz, nphi)


def solution(mesh):
    in_specs = (P("rad", None, "col", None), P("rad", "col", None), P(None, None, "rad"), P("rad"))
    out_specs = P("rad", None, "col", None)
    return jax.shard_map(
        on_device, mesh=mesh, in_specs=in_specs, out_specs=out_specs, check_vma=False
    )
```

```python
import jax
import jax.numpy as jnp
from jax import lax
from jax.experimental import pallas as pl
from jax.experimental.pallas import tpu as pltpu
from jax.sharding import PartitionSpec as P

SECTIONS = 2
GROUPS = 2
PARTS = 1
RATE_ROWS = 8
PIECES = 4

diffusion_coeff = 0.2
advection_coeff = 0.15
rotation_coeff = 0.25

F32 = jnp.float32
BF16 = jnp.bfloat16
MB = 1 << 20


def shape(dims, dtype=F32):
    return jax.ShapeDtypeStruct(dims, dtype)


def cost(flops, moved):
    return pl.CostEstimate(flops=int(flops), bytes_accessed=int(moved), transcendentals=0)


def params(limit=40):
    return pltpu.CompilerParams(vmem_limit_bytes=limit * MB)


def stencil(cur, upper, lower, other, state):
    up = diffusion_coeff - advection_coeff * state
    down = diffusion_coeff + advection_coeff * state
    out = (1.0 - 2.0 * diffusion_coeff) * cur + up * upper + down * lower
    return out if other is None else out + other


def split(values):
    high = values.astype(BF16)
    return high, (values - high.astype(F32)).astype(BF16)


def product(x_parts, h_high, h_low):
    pairs = [split(x) for x in x_parts]
    high = jnp.concatenate([p[0] for p in pairs], axis=1)
    low = jnp.concatenate([p[1] for p in pairs], axis=1)

    def dot(a, b):
        return jnp.dot(a, b, preferred_element_type=F32)

    return dot(high, h_high) + (dot(high, h_low) + dot(low, h_high))


def state_kernel(where, state, *refs, modes, nz):
    out = refs[-1]
    width = state.shape[1]
    rows = nz * width
    for z in range(nz):
        out[z * width : (z + 1) * width, :] = state[pl.ds(z, modes, stride=nz), :].T
    if len(refs) > 1:
        rate, helm = refs[:2]
        out[rows : rows + RATE_ROWS, :] = jnp.broadcast_to(rate[...], (RATE_ROWS, modes))
        out[rows + RATE_ROWS :, :] = helm[...].reshape(-1, modes)


def turn_state(where, state, foreign, rate=None, helm=None):
    modes, nz, nphi = state.shape
    half = nphi // 2
    side = (lambda i, w: (0, 1 - (w[0] >> 1))) if foreign else (lambda i, w: (0, w[0] >> 1))
    rows, more, more_specs = nz * half, (), []
    if helm is not None:
        comps = helm.shape[0]
        rows += RATE_ROWS + comps * modes
        more = (rate, helm)
        more_specs = [
            pl.BlockSpec((1, modes), lambda i, w: (0, 0)),
            pl.BlockSpec((comps, modes, modes), lambda i, w: (0, w[1], 0)),
        ]
    return pl.pallas_call(
        lambda *refs: state_kernel(*refs, modes=modes, nz=nz),
        out_shape=shape((rows, modes)),
        grid_spec=pltpu.PrefetchScalarGridSpec(
            num_scalar_prefetch=1,
            grid=(1,),
            in_specs=[pl.BlockSpec((modes * nz, half), side)] + more_specs,
            out_specs=pl.BlockSpec((rows, modes), lambda i, w: (0, 0)),
        ),
        compiler_params=params(16),
        cost_estimate=cost(rows * modes, 8 * rows * modes),
        name="turn_state",
    )(where, state.reshape(modes * nz, nphi), *more)


def edge_kernel(where, cot, leading, last, *, modes, nz):
    for c in range(3):
        at = slice(c * modes, (c + 1) * modes)
        leading[at, :] = cot[pl.ds(c * nz, modes, stride=3 * nz), :]
        last[at, :] = cot[pl.ds(c * nz + nz - 1, modes, stride=3 * nz), :]


def edge_layers(where, cot, foreign):
    modes, comps, nz, nphi = cot.shape
    half = nphi // 2
    side = (lambda i, w: (0, 1 - (w[0] >> 1))) if foreign else (lambda i, w: (0, w[0] >> 1))
    return pl.pallas_call(
        lambda *refs: edge_kernel(*refs, modes=modes, nz=nz),
        out_shape=[shape((comps * modes, half))] * 2,
        grid_spec=pltpu.PrefetchScalarGridSpec(
            num_scalar_prefetch=1,
            grid=(1,),
            in_specs=[pl.BlockSpec((modes * comps * nz, half), side)],
            out_specs=[pl.BlockSpec((comps * modes, half), lambda i, w: (0, 0))] * 2,
        ),
        compiler_params=params(16),
        cost_estimate=cost(modes * comps * nphi, 4 * modes * comps * nz * half),
        name="edge_layers",
    )(where, cot.reshape(modes * comps * nz, nphi))


def blanks(*like):
    return pl.pallas_call(
        lambda *outs: None,
        out_shape=[shape(dims, dtype) for dims, dtype in like],
        out_specs=[pl.BlockSpec(memory_space=pl.ANY)] * len(like),
        name="blanks",
    )()


def first_kernel(where, cot, state, after, before, rate, *rest, modes, nz, chunks):
    outs, turned = rest[:-1], rest[-1]
    half = cot.shape[1]
    width = half // chunks
    for c in range(3):
        turned[c, 0] = before[c * modes : (c + 1) * modes, :].T
        for z in range(nz):
            turned[c, z + 1] = cot[pl.ds(c * nz + z, modes, stride=3 * nz), :].T
        turned[c, nz + 1] = after[c * modes : (c + 1) * modes, :].T
    turn = rotation_coeff * rate[...]
    for z in range(nz):
        for k in range(chunks):
            at = slice(k * width, (k + 1) * width)
            st = state[z * half + k * width : z * half + (k + 1) * width, :]
            cur = [turned[c, z + 1, at, :] for c in range(3)]
            others = (turn * cur[1], -turn * cur[0], None)
            for c in range(3):
                outs[k][c, z] = stencil(cur[c], turned[c, z + 2, at, :], turned[c, z, at, :], others[c], st)


def first_stencil(where, cot, state_turned, after, before, rate, foreign, chunks):
    modes, comps, nz, nphi = cot.shape
    half = nphi // 2
    side = (lambda i, w: (0, 1 - (w[0] >> 1))) if foreign else (lambda i, w: (0, w[0] >> 1))
    whole = lambda i, w: (0, 0)
    out = (comps, nz, half // chunks, modes)
    return pl.pallas_call(
        lambda *refs: first_kernel(*refs, modes=modes, nz=nz, chunks=chunks),
        out_shape=[shape(out)] * chunks,
        grid_spec=pltpu.PrefetchScalarGridSpec(
            num_scalar_prefetch=1,
            grid=(1,),
            in_specs=[
                pl.BlockSpec((modes * comps * nz, half), side),
                pl.BlockSpec((nz * half, modes), whole),
                pl.BlockSpec((comps * modes, half), whole),
                pl.BlockSpec((comps * modes, half), whole),
                pl.BlockSpec((1, modes), whole),
            ],
            out_specs=[pl.BlockSpec(out, lambda i, w: (0, 0, 0, 0))] * chunks,
            scratch_shapes=[pltpu.VMEM((comps, nz + 2, half, modes), F32)],
        ),
        compiler_params=params(32),
        cost_estimate=cost(12 * modes * comps * nz * half, 8 * modes * comps * nz * half),
        name="first_stencil",
    )(where, cot.reshape(modes * comps * nz, nphi), state_turned, after, before, rate)


def helm_kernel(where, own, *refs):
    far, (high, low) = refs[:-2], refs[-2:]
    rows, modes = own.shape[1:]
    k = pl.program_id(0)
    wanted = block_of(k, where) ^ where[1]
    h, l = split(own[...])
    high[:, :, :modes] = h
    low[:, :, :modes] = l
    for d, ref in enumerate(far):

        @pl.when(wanted == d)
        def _(ref=ref):
            h, l = split(ref[...])
            high[:, :, modes:] = h
            low[:, :, modes:] = l


def block_of(k, where):
    return where[0] ^ (((k & 1) << 1) | (k >> 1))


def split_helm(where, own, far):
    comps, rows, modes = own.shape
    out = (comps, rows, 2 * modes)
    return pl.pallas_call(
        helm_kernel,
        out_shape=[shape(out, BF16)] * 2,
        grid_spec=pltpu.PrefetchScalarGridSpec(
            num_scalar_prefetch=1,
            grid=(rows // modes,),
            in_specs=[pl.BlockSpec((comps, modes, modes), lambda k, w: (0, block_of(k, w), 0))]
            + [pl.BlockSpec((comps, modes, modes), lambda k, w: (0, 0, 0))] * len(far),
            out_specs=[pl.BlockSpec((comps, modes, 2 * modes), lambda k, w: (0, k, 0))] * 2,
        ),
        compiler_params=params(16),
        cost_estimate=cost(4 * comps * rows * modes, 16 * comps * rows * modes),
        name="split_helm",
    )(where, own, *far)


def map1_kernel(own, far, own_peer, far_peer, high, low, out, first, last):
    _, nz, width, modes = own.shape
    rows = nz * width
    parts = [ref[0].reshape(rows, modes) for ref in (own, far, own_peer, far_peer)]
    res = product(parts, high[0], low[0]).reshape(nz, width, high.shape[2])
    out[0] = res
    first[0] = res[0]
    last[0] = res[nz - 1]


def map1(own, far, own_peer, far_peer, high, low, k):
    comps, nz, width, modes = far.shape
    width //= PARTS
    rows, cols = high.shape[1:]
    here = pl.BlockSpec((1, nz, width, modes), lambda c: (c, 0, k, 0))
    chunk = pl.BlockSpec((1, nz, width, modes), lambda c: (c, 0, k % PARTS, 0))
    helm = pl.BlockSpec((1, rows, cols), lambda c: (c, 0, 0))
    layer = pl.BlockSpec((1, width, cols), lambda c: (c, 0, 0))
    return pl.pallas_call(
        map1_kernel,
        out_shape=[shape((comps, nz, width, cols)), shape((comps, width, cols)), shape((comps, width, cols))],
        grid=(comps,),
        in_specs=[here, chunk, here, chunk, helm, helm],
        out_specs=[pl.BlockSpec((1, nz, width, cols), lambda c: (c, 0, 0, 0)), layer, layer],
        compiler_params=params(24),
        cost_estimate=cost(6 * comps * nz * width * rows * cols, 4 * comps * (nz * width * (rows + cols) + rows * cols)),
        name=f"map1_{k}",
    )(own, far, own_peer, far_peer, high, low)


def second_kernel(cur, after, before, state_own, state_far, rate, out, *, k, half):
    comps, nz, width, cols = cur.shape
    modes = cols // 2
    rates = (rate[...], state_far[nz * half : nz * half + 1, :])
    for g in range(2):
        lanes = slice(g * modes, (g + 1) * modes)
        turn = rotation_coeff * rates[g]
        state = (state_own, state_far)[g]
        for z in range(nz):
            st = state[z * half + k * width : z * half + (k + 1) * width, :]
            here = [cur[c, z, :, lanes] for c in range(comps)]
            others = (turn * here[1], -turn * here[0], None)
            for c in range(comps):
                upper = cur[c, z + 1, :, lanes] if z + 1 < nz else after[c, :, lanes]
                lower = cur[c, z - 1, :, lanes] if z else before[c, :, lanes]
                out[c, z, :, lanes] = stencil(here[c], upper, lower, others[c], st)


def second_stencil(cur, after, before, state_own, state_far, rate, k, half):
    return pl.pallas_call(
        lambda *refs: second_kernel(*refs, k=k, half=half),
        out_shape=shape(cur.shape),
        compiler_params=params(16),
        cost_estimate=cost(12 * cur.size, 8 * cur.size),
        name=f"second_stencil_{k}",
    )(cur, after, before, state_own, state_far, rate)


def map2_kernel(own, peer, high, low, *refs):
    out_own, out_far = refs[-2:]
    _, nz, width, cols = own.shape
    parts = [ref[0].reshape(nz * width, cols) for ref in (own, peer)]
    res = product(parts, high[0], low[0]).reshape(nz, width, cols)
    out_own[0] = res[:, :, : cols // 2]
    out_far[0] = res[:, :, cols // 2 :]


def map2(own, peer, high, low, k, base):
    comps, nz, width, cols = own.shape
    rows = high.shape[1]
    chunk = pl.BlockSpec((1, nz, width, cols), lambda c: (c, 0, 0, 0))
    helm = pl.BlockSpec((1, rows, cols), lambda c: (c, 0, 0))
    out = (comps, nz, width * PARTS, cols // 2)
    return pl.pallas_call(
        map2_kernel,
        out_shape=[shape(out)] * 2,
        grid=(comps,),
        in_specs=[chunk, chunk, helm, helm] + [pl.BlockSpec(memory_space=pl.ANY)] * len(base),
        out_specs=[pl.BlockSpec((1, nz, width, cols // 2), lambda c: (c, 0, k % PARTS, 0))] * 2,
        input_output_aliases={4 + i: i for i in range(len(base))},
        compiler_params=params(24),
        cost_estimate=cost(6 * comps * nz * width * rows * cols, 4 * comps * (nz * width * (rows + cols) + rows * cols)),
        name=f"map2_{k}",
    )(own, peer, high, low, *base)


def last_kernel(where, *refs, nz, chunks):
    ins, out = refs[:chunks], refs[-1]
    modes, _, width = out.shape
    rows = out.reshape(modes * nz, width)
    for z in range(nz):
        whole = jnp.concatenate([ref[0, z] for ref in ins], axis=0)
        rows[pl.ds(z, modes, stride=nz), :] = whole.T


def write_half(where, pieces, nphi, foreign, base=None):
    comps, nz, width, modes = pieces[0].shape
    chunks = len(pieces)
    side = (lambda c, w: (0, c, 1 - (w[0] >> 1))) if foreign else (lambda c, w: (0, c, w[0] >> 1))
    extra = () if base is None else (base,)
    return pl.pallas_call(
        lambda *refs: last_kernel(*refs, nz=nz, chunks=chunks),
        out_shape=shape((modes, comps * nz, nphi)),
        grid_spec=pltpu.PrefetchScalarGridSpec(
            num_scalar_prefetch=1,
            grid=(comps,),
            in_specs=[pl.BlockSpec((1,) + p.shape[1:], lambda c, w: (c, 0, 0, 0)) for p in pieces]
            + [pl.BlockSpec(memory_space=pl.ANY)] * len(extra),
            out_specs=pl.BlockSpec((modes, nz, nphi // 2), side),
        ),
        input_output_aliases={1 + chunks: 0} if extra else {},
        compiler_params=params(24),
        cost_estimate=cost(comps * nz * modes * nphi, 4 * comps * nz * modes * nphi),
        name="write_foreign" if foreign else "write_own",
    )(where, *pieces, *extra)


def tied(value, *others):
    return lax.optimization_barrier((value, *others))[0]


def on_device(cotangent, state_axial, helm_inverse, rotation_rate):
    modes, comps, nz, nphi = cotangent.shape
    half = nphi // 2
    peers, cols = lax.axis_size("rad"), lax.axis_size("col")
    up = [(i, (i + 1) % cols) for i in range(cols)]
    down = [(j, i) for i, j in up]

    def across(array):
        return lax.ppermute(array, "rad", [(i, i ^ 2) for i in range(peers)])

    def beside(array):
        return lax.ppermute(array, "rad", [(i, i ^ 1) for i in range(peers)])

    def hop(array, mask):
        return lax.ppermute(array, "col", [(i, i ^ mask) for i in range(cols)])

    lot = lax.axis_index("col").astype(jnp.int32) & (PIECES - 1)
    where = jnp.stack([lax.axis_index("rad").astype(jnp.int32), lot])
    rate = rotation_rate.reshape(1, modes)

    once = 1 + (where[0] >> 8)

    state_foreign = turn_state(where, state_axial, True, rate, helm_inverse)
    state_far = across(state_foreign)

    def halos(leading, last):
        return lax.ppermute(leading, "col", down), lax.ppermute(last, "col", up)

    def foreign_half(step, sent):
        here = where + (step >> 8)
        edges = halos(*edge_layers(here, cotangent, True))
        return tuple(first_stencil(here, cotangent, state_foreign, *edges, rate, True, GROUPS))

    chunk = (comps, nz, half // GROUPS, modes)
    sent = lax.fori_loop(0, once, foreign_half, tuple(blanks(*[(chunk, F32)] * GROUPS)))
    far = [across(tied(s, state_far) if k else s) for k, s in enumerate(sent)]

    def own_half(step, carry):
        here = where + (step >> 8)
        edges = halos(*edge_layers(here, entry, False))
        blocks = [tied(state_far, here)[nz * half + RATE_ROWS :].reshape(comps, modes, modes)]
        blocks += [hop(blocks[0], 1), hop(blocks[0], 2)]
        blocks += [hop(blocks[2], 1)]
        edges = tuple(tied(e, *blocks[1:]) for e in edges)
        state_own = turn_state(here, state_axial, False)
        (own,) = first_stencil(here, entry, state_own, *edges, rate, False, 1)
        own_peer = beside(own)
        return (state_own, own, own_peer, *split_helm(here, helm_inverse, blocks))

    entry = tied(cotangent, sent[0], state_far)
    columns = (comps, nz, half, modes)
    helm = (comps, peers * modes, 2 * modes)
    state_own, own, own_peer, high, low = lax.fori_loop(
        0, once, own_half, tuple(blanks(((nz * half, modes), F32), (columns, F32), (columns, F32), (helm, BF16), (helm, BF16)))
    )

    kept, back = [], []
    for g in range(GROUPS):
        group = range(g * PARTS, (g + 1) * PARTS)

        def chains(_, carry, group=group):
            here = carry[0]
            there = beside(here)
            moved = []
            for k in group:
                cur, leading, last = map1(own, here, own_peer, there, high, low, k)
                moved.append((cur, *halos(leading, last)))
            moved = lax.optimization_barrier(tuple(moved))
            nxt = [second_stencil(*m, state_own, state_far, rate, k, half) for k, m in zip(group, moved)]
            there = [beside(n) for n in nxt]
            mine_theirs = ()
            for k, n, t in zip(group, nxt, there):
                mine_theirs = tuple(map2(n, t, high, low, k, mine_theirs))
            return mine_theirs[::-1]

        spare = tied(sent[g], kept[-1]) if kept else sent[g]
        theirs, mine = lax.fori_loop(0, once, chains, (far[g], spare))
        kept.append(mine)
        back.append(across(theirs))
    out = write_half(where, kept, nphi, False)
    out = write_half(where, back, nphi, True, out)
    return out.reshape(modes, comps, nz, nphi)


def solution(mesh):
    in_specs = (P("rad", None, "col", None), P("rad", "col", None), P(None, None, "rad"), P("rad"))
    out_specs = P("rad", None, "col", None)
    return jax.shard_map(
        on_device, mesh=mesh, in_specs=in_specs, out_specs=out_specs, check_vma=False
    )
```

```python
import jax
import jax.numpy as jnp
from jax import lax
from jax.experimental import pallas as pl
from jax.experimental.pallas import tpu as pltpu
from jax.sharding import PartitionSpec as P

SECTIONS = 2
GROUPS = 2
PIECES_BACK = 3
RATE_ROWS = 8
PIECES = 4

diffusion_coeff = 0.2
advection_coeff = 0.15
rotation_coeff = 0.25

F32 = jnp.float32
BF16 = jnp.bfloat16
MB = 1 << 20


def shape(dims, dtype=F32):
    return jax.ShapeDtypeStruct(dims, dtype)


def cost(flops, moved):
    return pl.CostEstimate(flops=int(flops), bytes_accessed=int(moved), transcendentals=0)


def params(limit=40):
    return pltpu.CompilerParams(vmem_limit_bytes=limit * MB)


def stencil(cur, upper, lower, other, state):
    up = diffusion_coeff - advection_coeff * state
    down = diffusion_coeff + advection_coeff * state
    out = (1.0 - 2.0 * diffusion_coeff) * cur + up * upper + down * lower
    return out if other is None else out + other


def split(values):
    high = values.astype(BF16)
    return high, (values - high.astype(F32)).astype(BF16)


def product(x_parts, h_high, h_low):
    pairs = [split(x) for x in x_parts]
    high = jnp.concatenate([p[0] for p in pairs], axis=1)
    low = jnp.concatenate([p[1] for p in pairs], axis=1)

    def dot(a, b):
        return jnp.dot(a, b, preferred_element_type=F32)

    return dot(high, h_high) + (dot(high, h_low) + dot(low, h_high))


def state_kernel(where, state, *refs, modes, nz):
    out = refs[-1]
    width = state.shape[1]
    rows = nz * width
    for z in range(nz):
        out[z * width : (z + 1) * width, :] = state[pl.ds(z, modes, stride=nz), :].T
    if len(refs) > 1:
        out[rows:, :] = jnp.broadcast_to(refs[0][...], (RATE_ROWS, modes))


def turn_state(where, state, foreign, rate=None):
    modes, nz, nphi = state.shape
    half = nphi // 2
    side = (lambda i, w: (0, 1 - (w[0] >> 1))) if foreign else (lambda i, w: (0, w[0] >> 1))
    rows, more, more_specs = nz * half, (), []
    if rate is not None:
        rows += RATE_ROWS
        more = (rate,)
        more_specs = [pl.BlockSpec((1, modes), lambda i, w: (0, 0))]
    return pl.pallas_call(
        lambda *refs: state_kernel(*refs, modes=modes, nz=nz),
        out_shape=shape((rows, modes)),
        grid_spec=pltpu.PrefetchScalarGridSpec(
            num_scalar_prefetch=1,
            grid=(1,),
            in_specs=[pl.BlockSpec((modes * nz, half), side)] + more_specs,
            out_specs=pl.BlockSpec((rows, modes), lambda i, w: (0, 0)),
        ),
        compiler_params=params(16),
        cost_estimate=cost(rows * modes, 8 * rows * modes),
        name="turn_state",
    )(where, state.reshape(modes * nz, nphi), *more)


def edge_kernel(where, cot, leading, last, *, modes, nz):
    for c in range(3):
        at = slice(c * modes, (c + 1) * modes)
        leading[at, :] = cot[pl.ds(c * nz, modes, stride=3 * nz), :]
        last[at, :] = cot[pl.ds(c * nz + nz - 1, modes, stride=3 * nz), :]


def edge_layers(where, cot, foreign):
    modes, comps, nz, nphi = cot.shape
    half = nphi // 2
    side = (lambda i, w: (0, 1 - (w[0] >> 1))) if foreign else (lambda i, w: (0, w[0] >> 1))
    return pl.pallas_call(
        lambda *refs: edge_kernel(*refs, modes=modes, nz=nz),
        out_shape=[shape((comps * modes, half))] * 2,
        grid_spec=pltpu.PrefetchScalarGridSpec(
            num_scalar_prefetch=1,
            grid=(1,),
            in_specs=[pl.BlockSpec((modes * comps * nz, half), side)],
            out_specs=[pl.BlockSpec((comps * modes, half), lambda i, w: (0, 0))] * 2,
        ),
        compiler_params=params(16),
        cost_estimate=cost(modes * comps * nphi, 4 * modes * comps * nz * half),
        name="edge_layers",
    )(where, cot.reshape(modes * comps * nz, nphi))


def blanks(*like):
    return pl.pallas_call(
        lambda *outs: None,
        out_shape=[shape(dims, dtype) for dims, dtype in like],
        out_specs=[pl.BlockSpec(memory_space=pl.ANY)] * len(like),
        name="blanks",
    )()


def first_kernel(where, cot, state, after, before, rate, *rest, modes, nz, chunks):
    outs, turned = rest[:-1], rest[-1]
    half = cot.shape[1]
    width = half // chunks
    for c in range(3):
        turned[c, 0] = before[c * modes : (c + 1) * modes, :].T
        for z in range(nz):
            turned[c, z + 1] = cot[pl.ds(c * nz + z, modes, stride=3 * nz), :].T
        turned[c, nz + 1] = after[c * modes : (c + 1) * modes, :].T
    turn = rotation_coeff * rate[...]
    for z in range(nz):
        for k in range(chunks):
            at = slice(k * width, (k + 1) * width)
            st = state[z * half + k * width : z * half + (k + 1) * width, :]
            cur = [turned[c, z + 1, at, :] for c in range(3)]
            others = (turn * cur[1], -turn * cur[0], None)
            for c in range(3):
                outs[k][c, z] = stencil(cur[c], turned[c, z + 2, at, :], turned[c, z, at, :], others[c], st)


def first_stencil(where, cot, state_turned, after, before, rate, foreign, chunks):
    modes, comps, nz, nphi = cot.shape
    half = nphi // 2
    side = (lambda i, w: (0, 1 - (w[0] >> 1))) if foreign else (lambda i, w: (0, w[0] >> 1))
    whole = lambda i, w: (0, 0)
    out = (comps, nz, half // chunks, modes)
    return pl.pallas_call(
        lambda *refs: first_kernel(*refs, modes=modes, nz=nz, chunks=chunks),
        out_shape=[shape(out)] * chunks,
        grid_spec=pltpu.PrefetchScalarGridSpec(
            num_scalar_prefetch=1,
            grid=(1,),
            in_specs=[
                pl.BlockSpec((modes * comps * nz, half), side),
                pl.BlockSpec((nz * half, modes), whole),
                pl.BlockSpec((comps * modes, half), whole),
                pl.BlockSpec((comps * modes, half), whole),
                pl.BlockSpec((1, modes), whole),
            ],
            out_specs=[pl.BlockSpec(out, lambda i, w: (0, 0, 0, 0))] * chunks,
            scratch_shapes=[pltpu.VMEM((comps, nz + 2, half, modes), F32)],
        ),
        compiler_params=params(32),
        cost_estimate=cost(12 * modes * comps * nz * half, 8 * modes * comps * nz * half),
        name="first_stencil",
    )(where, cot.reshape(modes * comps * nz, nphi), state_turned, after, before, rate)


def helm_kernel(where, own, *refs):
    far, (high, low) = refs[:-2], refs[-2:]
    rows, modes = own.shape[1:]
    k = pl.program_id(0)
    wanted = block_of(k, where) ^ where[1]
    h, l = split(own[...])
    high[:, :, :modes] = h
    low[:, :, :modes] = l
    for d, ref in enumerate(far):

        @pl.when(wanted == d)
        def _(ref=ref):
            h, l = split(ref[...])
            high[:, :, modes:] = h
            low[:, :, modes:] = l


def block_of(k, where):
    return where[0] ^ (((k & 1) << 1) | (k >> 1))


def split_helm(where, own, far):
    comps, rows, modes = own.shape
    out = (comps, rows, 2 * modes)
    return pl.pallas_call(
        helm_kernel,
        out_shape=[shape(out, BF16)] * 2,
        grid_spec=pltpu.PrefetchScalarGridSpec(
            num_scalar_prefetch=1,
            grid=(rows // modes,),
            in_specs=[pl.BlockSpec((comps, modes, modes), lambda k, w: (0, block_of(k, w), 0))]
            + [pl.BlockSpec((comps, modes, modes), lambda k, w: (0, 0, 0))] * len(far),
            out_specs=[pl.BlockSpec((comps, modes, 2 * modes), lambda k, w: (0, k, 0))] * 2,
        ),
        compiler_params=params(16),
        cost_estimate=cost(4 * comps * rows * modes, 16 * comps * rows * modes),
        name="split_helm",
    )(where, own, *far)


def map1_kernel(own, far, own_peer, far_peer, high, low, out, first, last):
    _, nz, width, modes = own.shape
    rows = nz * width
    parts = [ref[0].reshape(rows, modes) for ref in (own, far, own_peer, far_peer)]
    res = product(parts, high[0], low[0]).reshape(nz, width, high.shape[2])
    out[0] = res
    first[0] = res[0]
    last[0] = res[nz - 1]


def map1(own, far, own_peer, far_peer, high, low, k):
    comps, nz, width, modes = far.shape
    rows, cols = high.shape[1:]
    here = pl.BlockSpec((1, nz, width, modes), lambda c: (c, 0, k, 0))
    chunk = pl.BlockSpec((1, nz, width, modes), lambda c: (c, 0, 0, 0))
    helm = pl.BlockSpec((1, rows, cols), lambda c: (c, 0, 0))
    layer = pl.BlockSpec((1, width, cols), lambda c: (c, 0, 0))
    return pl.pallas_call(
        map1_kernel,
        out_shape=[shape((comps, nz, width, cols)), shape((comps, width, cols)), shape((comps, width, cols))],
        grid=(comps,),
        in_specs=[here, chunk, here, chunk, helm, helm],
        out_specs=[pl.BlockSpec((1, nz, width, cols), lambda c: (c, 0, 0, 0)), layer, layer],
        compiler_params=params(24),
        cost_estimate=cost(6 * comps * nz * width * rows * cols, 4 * comps * (nz * width * (rows + cols) + rows * cols)),
        name=f"map1_{k}",
    )(own, far, own_peer, far_peer, high, low)


def second_kernel(cur, after, before, state_own, state_far, rate, out, *, k, half):
    comps, nz, width, cols = cur.shape
    modes = cols // 2
    rates = (rate[...], state_far[nz * half : nz * half + 1, :])
    for g in range(2):
        lanes = slice(g * modes, (g + 1) * modes)
        turn = rotation_coeff * rates[g]
        state = (state_own, state_far)[g]
        for z in range(nz):
            st = state[z * half + k * width : z * half + (k + 1) * width, :]
            here = [cur[c, z, :, lanes] for c in range(comps)]
            others = (turn * here[1], -turn * here[0], None)
            for c in range(comps):
                upper = cur[c, z + 1, :, lanes] if z + 1 < nz else after[c, :, lanes]
                lower = cur[c, z - 1, :, lanes] if z else before[c, :, lanes]
                out[c, z, :, lanes] = stencil(here[c], upper, lower, others[c], st)


def second_stencil(cur, after, before, state_own, state_far, rate, k, half):
    return pl.pallas_call(
        lambda *refs: second_kernel(*refs, k=k, half=half),
        out_shape=shape(cur.shape),
        compiler_params=params(16),
        cost_estimate=cost(12 * cur.size, 8 * cur.size),
        name=f"second_stencil_{k}",
    )(cur, after, before, state_own, state_far, rate)


def map2_kernel(own, peer, high, low, out_own, *outs_far):
    _, nz, width, cols = own.shape
    parts = [ref[0].reshape(nz * width, cols) for ref in (own, peer)]
    res = product(parts, high[0], low[0]).reshape(nz, width, cols)
    out_own[0] = res[:, :, : cols // 2]
    per = pl.num_programs(0) // len(outs_far)
    for i, out in enumerate(outs_far):

        @pl.when(pl.program_id(0) // per == i)
        def _(out=out):
            out[0] = res[:, :, cols // 2 :]


def map2(own, peer, high, low, k, pieces):
    comps, nz, width, cols = own.shape
    rows, per = high.shape[1], comps // pieces
    chunk = pl.BlockSpec((1, nz, width, cols), lambda c: (c, 0, 0, 0))
    helm = pl.BlockSpec((1, rows, cols), lambda c: (c, 0, 0))
    block = (1, nz, width, cols // 2)
    far = [pl.BlockSpec(block, lambda c, i=i: (jnp.clip(c - i * per, 0, per - 1), 0, 0, 0)) for i in range(pieces)]
    return pl.pallas_call(
        map2_kernel,
        out_shape=[shape((comps, *block[1:]))] + [shape((per, *block[1:]))] * pieces,
        grid=(comps,),
        in_specs=[chunk, chunk, helm, helm],
        out_specs=[pl.BlockSpec(block, lambda c: (c, 0, 0, 0)), *far],
        compiler_params=params(24),
        cost_estimate=cost(6 * comps * nz * width * rows * cols, 4 * comps * (nz * width * (rows + cols) + rows * cols)),
        name=f"map2_{k}",
    )(own, peer, high, low)


def last_kernel(where, *refs, nz, chunks):
    ins, out = refs[:chunks], refs[-1]
    modes, _, width = out.shape
    rows = out.reshape(modes * nz, width)
    for z in range(nz):
        whole = jnp.concatenate([ref[0, z] for ref in ins], axis=0)
        rows[pl.ds(z, modes, stride=nz), :] = whole.T


def write_half(where, pieces, nphi, foreign, base=None, first=0):
    count = min(p.shape[0] for p in pieces)
    comps = max(p.shape[0] for p in pieces)
    nz, _, modes = pieces[0].shape[1:]
    chunks = len(pieces)
    side = (lambda w: 1 - (w[0] >> 1)) if foreign else (lambda w: w[0] >> 1)
    extra = () if base is None else (base,)

    def spec(piece):
        begin = first if piece.shape[0] > count else 0
        return pl.BlockSpec((1, *piece.shape[1:]), lambda c, w: (begin + c, 0, 0, 0))

    return pl.pallas_call(
        lambda *refs: last_kernel(*refs, nz=nz, chunks=chunks),
        out_shape=shape((modes, comps * nz, nphi)),
        grid_spec=pltpu.PrefetchScalarGridSpec(
            num_scalar_prefetch=1,
            grid=(count,),
            in_specs=[spec(p) for p in pieces] + [pl.BlockSpec(memory_space=pl.ANY)] * len(extra),
            out_specs=pl.BlockSpec((modes, nz, nphi // 2), lambda c, w: (0, first + c, side(w))),
        ),
        input_output_aliases={1 + chunks: 0} if extra else {},
        compiler_params=params(24),
        cost_estimate=cost(count * nz * modes * nphi, 4 * count * nz * modes * nphi),
        name=f"write_foreign_{first}" if foreign else "write_own",
    )(where, *pieces, *extra)


def tied(value, *others):
    return lax.optimization_barrier((value, *others))[0]


def on_device(cotangent, state_axial, helm_inverse, rotation_rate):
    modes, comps, nz, nphi = cotangent.shape
    half = nphi // 2
    peers, cols = lax.axis_size("rad"), lax.axis_size("col")
    up = [(i, (i + 1) % cols) for i in range(cols)]
    down = [(j, i) for i, j in up]

    def across(array):
        return lax.ppermute(array, "rad", [(i, i ^ 2) for i in range(peers)])

    def beside(array):
        return lax.ppermute(array, "rad", [(i, i ^ 1) for i in range(peers)])

    def hop(array, mask):
        return lax.ppermute(array, "col", [(i, i ^ mask) for i in range(cols)])

    lot = lax.axis_index("col").astype(jnp.int32) & (PIECES - 1)
    where = jnp.stack([lax.axis_index("rad").astype(jnp.int32), lot])
    rate = rotation_rate.reshape(1, modes)

    once = 1 + (where[0] >> 8)

    piece = across(lax.dynamic_slice_in_dim(helm_inverse, lot * modes, modes, axis=1))
    state_foreign = turn_state(where, state_axial, True, rate)
    state_far = across(state_foreign)

    def halos(leading, last):
        return lax.ppermute(leading, "col", down), lax.ppermute(last, "col", up)

    def foreign_half(step, _):
        here = where + (step >> 8)
        edges = halos(*edge_layers(here, cotangent, True))
        blocks = [tied(piece, here)]
        blocks += [hop(blocks[0], 1), hop(blocks[0], 2)]
        blocks += [hop(blocks[2], 1)]
        return (*first_stencil(here, cotangent, state_foreign, *edges, rate, True, GROUPS), *blocks[1:])

    chunk = (comps, nz, half // GROUPS, modes)
    block = (comps, modes, modes)
    sent = lax.fori_loop(0, once, foreign_half, tuple(blanks(*[(chunk, F32)] * GROUPS, *[(block, F32)] * (PIECES - 1))))
    sent, blocks = sent[:GROUPS], [piece, *sent[GROUPS:]]
    far = [across(tied(s, state_far) if k else tied(s, piece)) for k, s in enumerate(sent)]

    def own_half(step, carry):
        here = where + (step >> 8)
        edges = halos(*edge_layers(here, entry, False))
        state_own = turn_state(here, state_axial, False)
        (own,) = first_stencil(here, entry, state_own, *edges, rate, False, 1)
        own_peer = beside(own)
        return (state_own, own, own_peer, *split_helm(here, helm_inverse, blocks))

    entry = tied(cotangent, sent[0])
    columns = (comps, nz, half, modes)
    helm = (comps, peers * modes, 2 * modes)
    state_own, own, own_peer, high, low = lax.fori_loop(
        0, once, own_half, tuple(blanks(((nz * half, modes), F32), (columns, F32), (columns, F32), (helm, BF16), (helm, BF16)))
    )

    kept, back = [], []
    width = half // GROUPS
    for k in range(GROUPS):
        pieces = PIECES_BACK if k == GROUPS - 1 else 1

        def chain(step, _, k=k, pieces=pieces):
            here = tied(far[k], step)
            cur, leading, last = map1(own, here, own_peer, beside(here), high, low, k)
            nxt = second_stencil(cur, *halos(leading, last), state_own, state_far, rate, k, half)
            return tuple(map2(nxt, beside(nxt), high, low, k, pieces))

        spare = tied(sent[k], kept[-1]) if kept else sent[k]
        parts = blanks(*[((comps // pieces, nz, width, modes), F32)] * pieces)
        mine, *theirs = lax.fori_loop(0, once, chain, (spare, *parts))
        kept.append(mine)
        back.append([across(t) for t in theirs])
    out = write_half(where, kept, nphi, False)
    for i in range(PIECES_BACK):
        group = [b[0] if len(b) == 1 else b[i] for b in back]
        out = write_half(where, group, nphi, True, out, i * (comps // PIECES_BACK))
    return out.reshape(modes, comps, nz, nphi)


def solution(mesh):
    in_specs = (P("rad", None, "col", None), P("rad", "col", None), P(None, None, "rad"), P("rad"))
    out_specs = P("rad", None, "col", None)
    return jax.shard_map(
        on_device, mesh=mesh, in_specs=in_specs, out_specs=out_specs, check_vma=False
    )
```

```python
import jax
import jax.numpy as jnp
from jax import lax
from jax.experimental import pallas as pl
from jax.experimental.pallas import tpu as pltpu
from jax.sharding import PartitionSpec as P

SECTIONS = 2
GROUPS = 2
PIECES_BACK = 3
RATE_ROWS = 8
PIECES = 4

diffusion_coeff = 0.2
advection_coeff = 0.15
rotation_coeff = 0.25

F32 = jnp.float32
BF16 = jnp.bfloat16
MB = 1 << 20


def shape(dims, dtype=F32):
    return jax.ShapeDtypeStruct(dims, dtype)


def cost(flops, moved):
    return pl.CostEstimate(flops=int(flops), bytes_accessed=int(moved), transcendentals=0)


def params(limit=40):
    return pltpu.CompilerParams(vmem_limit_bytes=limit * MB)


def stencil(cur, upper, lower, other, state):
    up = diffusion_coeff - advection_coeff * state
    down = diffusion_coeff + advection_coeff * state
    out = (1.0 - 2.0 * diffusion_coeff) * cur + up * upper + down * lower
    return out if other is None else out + other


def split(values):
    high = values.astype(BF16)
    return high, (values - high.astype(F32)).astype(BF16)


def product(x_parts, h_high, h_low):
    pairs = [split(x) for x in x_parts]
    high = jnp.concatenate([p[0] for p in pairs], axis=1)
    low = jnp.concatenate([p[1] for p in pairs], axis=1)

    def dot(a, b):
        return jnp.dot(a, b, preferred_element_type=F32)

    return dot(high, h_high) + (dot(high, h_low) + dot(low, h_high))


def state_kernel(where, state, *refs, modes, nz):
    out = refs[-1]
    width = state.shape[1]
    rows = nz * width
    for z in range(nz):
        out[z * width : (z + 1) * width, :] = state[pl.ds(z, modes, stride=nz), :].T
    if len(refs) > 1:
        out[rows:, :] = jnp.broadcast_to(refs[0][...], (RATE_ROWS, modes))


def turn_state(where, state, foreign, rate=None):
    modes, nz, nphi = state.shape
    half = nphi // 2
    side = (lambda i, w: (0, 1 - (w[0] >> 1))) if foreign else (lambda i, w: (0, w[0] >> 1))
    rows, more, more_specs = nz * half, (), []
    if rate is not None:
        rows += RATE_ROWS
        more = (rate,)
        more_specs = [pl.BlockSpec((1, modes), lambda i, w: (0, 0))]
    return pl.pallas_call(
        lambda *refs: state_kernel(*refs, modes=modes, nz=nz),
        out_shape=shape((rows, modes)),
        grid_spec=pltpu.PrefetchScalarGridSpec(
            num_scalar_prefetch=1,
            grid=(1,),
            in_specs=[pl.BlockSpec((modes * nz, half), side)] + more_specs,
            out_specs=pl.BlockSpec((rows, modes), lambda i, w: (0, 0)),
        ),
        compiler_params=params(16),
        cost_estimate=cost(rows * modes, 8 * rows * modes),
        name="turn_state",
    )(where, state.reshape(modes * nz, nphi), *more)


def edge_kernel(where, cot, leading, last, *, modes, nz):
    for c in range(3):
        at = slice(c * modes, (c + 1) * modes)
        leading[at, :] = cot[pl.ds(c * nz, modes, stride=3 * nz), :]
        last[at, :] = cot[pl.ds(c * nz + nz - 1, modes, stride=3 * nz), :]


def edge_layers(where, cot, foreign):
    modes, comps, nz, nphi = cot.shape
    half = nphi // 2
    side = (lambda i, w: (0, 1 - (w[0] >> 1))) if foreign else (lambda i, w: (0, w[0] >> 1))
    return pl.pallas_call(
        lambda *refs: edge_kernel(*refs, modes=modes, nz=nz),
        out_shape=[shape((comps * modes, half))] * 2,
        grid_spec=pltpu.PrefetchScalarGridSpec(
            num_scalar_prefetch=1,
            grid=(1,),
            in_specs=[pl.BlockSpec((modes * comps * nz, half), side)],
            out_specs=[pl.BlockSpec((comps * modes, half), lambda i, w: (0, 0))] * 2,
        ),
        compiler_params=params(16),
        cost_estimate=cost(modes * comps * nphi, 4 * modes * comps * nz * half),
        name="edge_layers",
    )(where, cot.reshape(modes * comps * nz, nphi))


def blanks(*like):
    return pl.pallas_call(
        lambda *outs: None,
        out_shape=[shape(dims, dtype) for dims, dtype in like],
        out_specs=[pl.BlockSpec(memory_space=pl.ANY)] * len(like),
        name="blanks",
    )()


def turn_kernel(where, cot, out, *, modes, nz, comps):
    for c in range(comps):
        for z in range(nz):
            out[c, z] = cot[pl.ds(c * nz + z, modes, stride=comps * nz), :].T


def turn_half(where, cot, foreign):
    modes, comps, nz, nphi = cot.shape
    half = nphi // 2
    side = (lambda i, w: (0, 1 - (w[0] >> 1))) if foreign else (lambda i, w: (0, w[0] >> 1))
    out = (comps, nz, half, modes)
    return pl.pallas_call(
        lambda *refs: turn_kernel(*refs, modes=modes, nz=nz, comps=comps),
        out_shape=shape(out),
        grid_spec=pltpu.PrefetchScalarGridSpec(
            num_scalar_prefetch=1,
            grid=(1,),
            in_specs=[pl.BlockSpec((modes * comps * nz, half), side)],
            out_specs=pl.BlockSpec(out, lambda i, w: (0, 0, 0, 0)),
        ),
        compiler_params=params(20),
        cost_estimate=cost(modes * comps * nz * half, 8 * modes * comps * nz * half),
        name="turn_half",
    )(where, cot.reshape(modes * comps * nz, nphi))


def first_kernel(turned, state, after, before, rate, *rest):
    outs, edges = rest[:-1], rest[-1]
    comps, nz, half, modes = turned.shape
    width = half // len(outs)
    for c in range(comps):
        edges[c, 0] = before[c * modes : (c + 1) * modes, :].T
        edges[c, 1] = after[c * modes : (c + 1) * modes, :].T
    turn = rotation_coeff * rate[...]
    step = 32
    for z in range(nz):
        for p in range(0, half, step):
            at = slice(p, p + step)
            st = state[z * half + p : z * half + p + step, :]
            cur = [turned[c, z, at, :] for c in range(comps)]
            others = (turn * cur[1], -turn * cur[0], None)
            for c in range(comps):
                upper = turned[c, z + 1, at, :] if z + 1 < nz else edges[c, 1, at, :]
                lower = turned[c, z - 1, at, :] if z else edges[c, 0, at, :]
                to = p % width
                outs[p // width][c, z, to : to + step, :] = stencil(cur[c], upper, lower, others[c], st)


def first_stencil(turned, state_turned, after, before, rate, chunks):
    comps, nz, half, modes = turned.shape
    out = (comps, nz, half // chunks, modes)
    return pl.pallas_call(
        first_kernel,
        out_shape=[shape(out)] * chunks,
        grid=(1,),
        in_specs=[
            pl.BlockSpec(turned.shape, lambda i: (0, 0, 0, 0)),
            pl.BlockSpec((nz * half, modes), lambda i: (0, 0)),
            pl.BlockSpec((comps * modes, half), lambda i: (0, 0)),
            pl.BlockSpec((comps * modes, half), lambda i: (0, 0)),
            pl.BlockSpec((1, modes), lambda i: (0, 0)),
        ],
        out_specs=[pl.BlockSpec(out, lambda i: (0, 0, 0, 0))] * chunks,
        scratch_shapes=[pltpu.VMEM((comps, 2, half, modes), F32)],
        compiler_params=params(32),
        cost_estimate=cost(12 * modes * comps * nz * half, 8 * modes * comps * nz * half),
        name="first_stencil",
    )(turned, state_turned, after, before, rate)


def helm_kernel(where, own, *refs):
    far, (high, low) = refs[:-2], refs[-2:]
    rows, modes = own.shape[1:]
    k = pl.program_id(0)
    wanted = block_of(k, where) ^ where[1]
    h, l = split(own[...])
    high[:, :, :modes] = h
    low[:, :, :modes] = l
    for d, ref in enumerate(far):

        @pl.when(wanted == d)
        def _(ref=ref):
            h, l = split(ref[...])
            high[:, :, modes:] = h
            low[:, :, modes:] = l


def block_of(k, where):
    return where[0] ^ (((k & 1) << 1) | (k >> 1))


def split_helm(where, own, far):
    comps, rows, modes = own.shape
    out = (comps, rows, 2 * modes)
    return pl.pallas_call(
        helm_kernel,
        out_shape=[shape(out, BF16)] * 2,
        grid_spec=pltpu.PrefetchScalarGridSpec(
            num_scalar_prefetch=1,
            grid=(rows // modes,),
            in_specs=[pl.BlockSpec((comps, modes, modes), lambda k, w: (0, block_of(k, w), 0))]
            + [pl.BlockSpec((comps, modes, modes), lambda k, w: (0, 0, 0))] * len(far),
            out_specs=[pl.BlockSpec((comps, modes, 2 * modes), lambda k, w: (0, k, 0))] * 2,
        ),
        compiler_params=params(16),
        cost_estimate=cost(4 * comps * rows * modes, 16 * comps * rows * modes),
        name="split_helm",
    )(where, own, *far)


def map1_kernel(own, far, own_peer, far_peer, high, low, out, first, last):
    _, nz, width, modes = own.shape
    rows = nz * width
    parts = [ref[0].reshape(rows, modes) for ref in (own, far, own_peer, far_peer)]
    res = product(parts, high[0], low[0]).reshape(nz, width, high.shape[2])
    out[0] = res
    first[0] = res[0]
    last[0] = res[nz - 1]


def map1(own, far, own_peer, far_peer, high, low, k):
    comps, nz, width, modes = far.shape
    rows, cols = high.shape[1:]
    here = pl.BlockSpec((1, nz, width, modes), lambda c: (c, 0, k, 0))
    chunk = pl.BlockSpec((1, nz, width, modes), lambda c: (c, 0, 0, 0))
    helm = pl.BlockSpec((1, rows, cols), lambda c: (c, 0, 0))
    layer = pl.BlockSpec((1, width, cols), lambda c: (c, 0, 0))
    return pl.pallas_call(
        map1_kernel,
        out_shape=[shape((comps, nz, width, cols)), shape((comps, width, cols)), shape((comps, width, cols))],
        grid=(comps,),
        in_specs=[here, chunk, here, chunk, helm, helm],
        out_specs=[pl.BlockSpec((1, nz, width, cols), lambda c: (c, 0, 0, 0)), layer, layer],
        compiler_params=params(24),
        cost_estimate=cost(6 * comps * nz * width * rows * cols, 4 * comps * (nz * width * (rows + cols) + rows * cols)),
        name=f"map1_{k}",
    )(own, far, own_peer, far_peer, high, low)


def second_kernel(cur, after, before, state_own, state_far, rate, out, *, k, half):
    comps, nz, width, cols = cur.shape
    modes = cols // 2
    rates = (rate[...], state_far[nz * half : nz * half + 1, :])
    for g in range(2):
        lanes = slice(g * modes, (g + 1) * modes)
        turn = rotation_coeff * rates[g]
        state = (state_own, state_far)[g]
        for z in range(nz):
            st = state[z * half + k * width : z * half + (k + 1) * width, :]
            here = [cur[c, z, :, lanes] for c in range(comps)]
            others = (turn * here[1], -turn * here[0], None)
            for c in range(comps):
                upper = cur[c, z + 1, :, lanes] if z + 1 < nz else after[c, :, lanes]
                lower = cur[c, z - 1, :, lanes] if z else before[c, :, lanes]
                out[c, z, :, lanes] = stencil(here[c], upper, lower, others[c], st)


def second_stencil(cur, after, before, state_own, state_far, rate, k, half):
    return pl.pallas_call(
        lambda *refs: second_kernel(*refs, k=k, half=half),
        out_shape=shape(cur.shape),
        compiler_params=params(16),
        cost_estimate=cost(12 * cur.size, 8 * cur.size),
        name=f"second_stencil_{k}",
    )(cur, after, before, state_own, state_far, rate)


def map2_kernel(own, peer, high, low, out_own, *outs_far):
    _, nz, width, cols = own.shape
    parts = [ref[0].reshape(nz * width, cols) for ref in (own, peer)]
    res = product(parts, high[0], low[0]).reshape(nz, width, cols)
    out_own[0] = res[:, :, : cols // 2]
    per = pl.num_programs(0) // len(outs_far)
    for i, out in enumerate(outs_far):

        @pl.when(pl.program_id(0) // per == i)
        def _(out=out):
            out[0] = res[:, :, cols // 2 :]


def map2(own, peer, high, low, k, pieces):
    comps, nz, width, cols = own.shape
    rows, per = high.shape[1], comps // pieces
    chunk = pl.BlockSpec((1, nz, width, cols), lambda c: (c, 0, 0, 0))
    helm = pl.BlockSpec((1, rows, cols), lambda c: (c, 0, 0))
    block = (1, nz, width, cols // 2)
    far = [pl.BlockSpec(block, lambda c, i=i: (jnp.clip(c - i * per, 0, per - 1), 0, 0, 0)) for i in range(pieces)]
    return pl.pallas_call(
        map2_kernel,
        out_shape=[shape((comps, *block[1:]))] + [shape((per, *block[1:]))] * pieces,
        grid=(comps,),
        in_specs=[chunk, chunk, helm, helm],
        out_specs=[pl.BlockSpec(block, lambda c: (c, 0, 0, 0)), *far],
        compiler_params=params(24),
        cost_estimate=cost(6 * comps * nz * width * rows * cols, 4 * comps * (nz * width * (rows + cols) + rows * cols)),
        name=f"map2_{k}",
    )(own, peer, high, low)


def last_kernel(where, *refs, nz, chunks):
    ins, out = refs[:chunks], refs[-1]
    modes, _, width = out.shape
    rows = out.reshape(modes * nz, width)
    for z in range(nz):
        whole = jnp.concatenate([ref[0, z] for ref in ins], axis=0)
        rows[pl.ds(z, modes, stride=nz), :] = whole.T


def write_half(where, pieces, nphi, foreign, base=None, first=0):
    count = min(p.shape[0] for p in pieces)
    comps = max(p.shape[0] for p in pieces)
    nz, _, modes = pieces[0].shape[1:]
    chunks = len(pieces)
    side = (lambda w: 1 - (w[0] >> 1)) if foreign else (lambda w: w[0] >> 1)
    extra = () if base is None else (base,)

    def spec(piece):
        begin = first if piece.shape[0] > count else 0
        return pl.BlockSpec((1, *piece.shape[1:]), lambda c, w: (begin + c, 0, 0, 0))

    return pl.pallas_call(
        lambda *refs: last_kernel(*refs, nz=nz, chunks=chunks),
        out_shape=shape((modes, comps * nz, nphi)),
        grid_spec=pltpu.PrefetchScalarGridSpec(
            num_scalar_prefetch=1,
            grid=(count,),
            in_specs=[spec(p) for p in pieces] + [pl.BlockSpec(memory_space=pl.ANY)] * len(extra),
            out_specs=pl.BlockSpec((modes, nz, nphi // 2), lambda c, w: (0, first + c, side(w))),
        ),
        input_output_aliases={1 + chunks: 0} if extra else {},
        compiler_params=params(24),
        cost_estimate=cost(count * nz * modes * nphi, 4 * count * nz * modes * nphi),
        name=f"write_foreign_{first}" if foreign else "write_own",
    )(where, *pieces, *extra)


def tied(value, *others):
    return lax.optimization_barrier((value, *others))[0]


def on_device(cotangent, state_axial, helm_inverse, rotation_rate):
    modes, comps, nz, nphi = cotangent.shape
    half = nphi // 2
    peers, cols = lax.axis_size("rad"), lax.axis_size("col")
    up = [(i, (i + 1) % cols) for i in range(cols)]
    down = [(j, i) for i, j in up]

    def across(array):
        return lax.ppermute(array, "rad", [(i, i ^ 2) for i in range(peers)])

    def beside(array):
        return lax.ppermute(array, "rad", [(i, i ^ 1) for i in range(peers)])

    def hop(array, mask):
        return lax.ppermute(array, "col", [(i, i ^ mask) for i in range(cols)])

    lot = lax.axis_index("col").astype(jnp.int32) & (PIECES - 1)
    where = jnp.stack([lax.axis_index("rad").astype(jnp.int32), lot])
    rate = rotation_rate.reshape(1, modes)

    once = 1 + (where[0] >> 8)

    piece = across(lax.dynamic_slice_in_dim(helm_inverse, lot * modes, modes, axis=1))
    state_foreign = turn_state(where, state_axial, True, rate)
    state_far = across(state_foreign)

    def halos(leading, last):
        return lax.ppermute(leading, "col", down), lax.ppermute(last, "col", up)

    def foreign_half(step, _):
        here = where + (step >> 8)
        edges = halos(*edge_layers(here, cotangent, True))
        blocks = [tied(piece, here)]
        blocks += [hop(blocks[0], 1), hop(blocks[0], 2)]
        return (*first_stencil(turn_half(here, cotangent, True), state_foreign, *edges, rate, GROUPS), *blocks[1:])

    chunk = (comps, nz, half // GROUPS, modes)
    block = (comps, modes, modes)
    sent = lax.fori_loop(0, once, foreign_half, tuple(blanks(*[(chunk, F32)] * GROUPS, *[(block, F32)] * (PIECES - 2))))
    sent, blocks = sent[:GROUPS], [piece, *sent[GROUPS:]]
    far = [across(tied(s, state_far) if k else tied(s, piece)) for k, s in enumerate(sent)]

    def own_half(step, carry):
        here = where + (step >> 8)
        edges = halos(*edge_layers(here, entry, False))
        last_block = hop(tied(blocks[2], here), 1)
        edges = tuple(tied(e, last_block) for e in edges)
        state_own = turn_state(here, state_axial, False)
        (own,) = first_stencil(turn_half(here, entry, False), state_own, *edges, rate, 1)
        own_peer = beside(own)
        return (state_own, own, own_peer, *split_helm(here, helm_inverse, [*blocks, last_block]))

    entry = tied(cotangent, sent[0])
    columns = (comps, nz, half, modes)
    helm = (comps, peers * modes, 2 * modes)
    state_own, own, own_peer, high, low = lax.fori_loop(
        0, once, own_half, tuple(blanks(((nz * half, modes), F32), (columns, F32), (columns, F32), (helm, BF16), (helm, BF16)))
    )

    kept, back = [], []
    width = half // GROUPS
    for k in range(GROUPS):
        pieces = PIECES_BACK if k == GROUPS - 1 else 1

        def chain(step, _, k=k, pieces=pieces):
            here = tied(far[k], step)
            cur, leading, last = map1(own, here, own_peer, beside(here), high, low, k)
            nxt = second_stencil(cur, *halos(leading, last), state_own, state_far, rate, k, half)
            return tuple(map2(nxt, beside(nxt), high, low, k, pieces))

        spare = tied(sent[k], kept[-1]) if kept else sent[k]
        parts = blanks(*[((comps // pieces, nz, width, modes), F32)] * pieces)
        mine, *theirs = lax.fori_loop(0, once, chain, (spare, *parts))
        kept.append(mine)
        back.append([across(t) for t in theirs])
    out = write_half(where, kept, nphi, False)
    for i in range(PIECES_BACK):
        group = [b[0] if len(b) == 1 else b[i] for b in back]
        out = write_half(where, group, nphi, True, out, i * (comps // PIECES_BACK))
    return out.reshape(modes, comps, nz, nphi)


def solution(mesh):
    in_specs = (P("rad", None, "col", None), P("rad", "col", None), P(None, None, "rad"), P("rad"))
    out_specs = P("rad", None, "col", None)
    return jax.shard_map(
        on_device, mesh=mesh, in_specs=in_specs, out_specs=out_specs, check_vma=False
    )
```

```python
import jax
import jax.numpy as jnp
from jax import lax
from jax.experimental import pallas as pl
from jax.experimental.pallas import tpu as pltpu
from jax.sharding import PartitionSpec as P

SECTIONS = 2
GROUPS = 2
PIECES_BACK = 3
RATE_ROWS = 8
PIECES = 4

diffusion_coeff = 0.2
advection_coeff = 0.15
rotation_coeff = 0.25

F32 = jnp.float32
BF16 = jnp.bfloat16
MB = 1 << 20


def shape(dims, dtype=F32):
    return jax.ShapeDtypeStruct(dims, dtype)


def cost(flops, moved):
    return pl.CostEstimate(flops=int(flops), bytes_accessed=int(moved), transcendentals=0)


def params(limit=40):
    return pltpu.CompilerParams(vmem_limit_bytes=limit * MB)


def stencil(cur, upper, lower, other, state):
    up = diffusion_coeff - advection_coeff * state
    down = diffusion_coeff + advection_coeff * state
    out = (1.0 - 2.0 * diffusion_coeff) * cur + up * upper + down * lower
    return out if other is None else out + other


def split(values):
    high = values.astype(BF16)
    return high, (values - high.astype(F32)).astype(BF16)


def product(x_parts, h_high, h_low):
    pairs = [split(x) for x in x_parts]
    high = jnp.concatenate([p[0] for p in pairs], axis=1)
    low = jnp.concatenate([p[1] for p in pairs], axis=1)

    def dot(a, b):
        return jnp.dot(a, b, preferred_element_type=F32)

    return dot(high, h_high) + (dot(high, h_low) + dot(low, h_high))


def state_kernel(where, state, *refs, modes, nz):
    out = refs[-1]
    width = state.shape[1]
    rows = nz * width
    for z in range(nz):
        out[z * width : (z + 1) * width, :] = state[pl.ds(z, modes, stride=nz), :].T
    if len(refs) > 1:
        out[rows:, :] = jnp.broadcast_to(refs[0][...], (RATE_ROWS, modes))


def turn_state(where, state, foreign, rate=None):
    modes, nz, nphi = state.shape
    half = nphi // 2
    side = (lambda i, w: (0, 1 - (w[0] >> 1))) if foreign else (lambda i, w: (0, w[0] >> 1))
    rows, more, more_specs = nz * half, (), []
    if rate is not None:
        rows += RATE_ROWS
        more = (rate,)
        more_specs = [pl.BlockSpec((1, modes), lambda i, w: (0, 0))]
    return pl.pallas_call(
        lambda *refs: state_kernel(*refs, modes=modes, nz=nz),
        out_shape=shape((rows, modes)),
        grid_spec=pltpu.PrefetchScalarGridSpec(
            num_scalar_prefetch=1,
            grid=(1,),
            in_specs=[pl.BlockSpec((modes * nz, half), side)] + more_specs,
            out_specs=pl.BlockSpec((rows, modes), lambda i, w: (0, 0)),
        ),
        compiler_params=params(16),
        cost_estimate=cost(rows * modes, 8 * rows * modes),
        name="turn_state",
    )(where, state.reshape(modes * nz, nphi), *more)


def edge_kernel(where, cot, leading, last, *, modes, nz):
    for c in range(3):
        at = slice(c * modes, (c + 1) * modes)
        leading[at, :] = cot[pl.ds(c * nz, modes, stride=3 * nz), :]
        last[at, :] = cot[pl.ds(c * nz + nz - 1, modes, stride=3 * nz), :]


def edge_layers(where, cot, foreign):
    modes, comps, nz, nphi = cot.shape
    half = nphi // 2
    side = (lambda i, w: (0, 1 - (w[0] >> 1))) if foreign else (lambda i, w: (0, w[0] >> 1))
    return pl.pallas_call(
        lambda *refs: edge_kernel(*refs, modes=modes, nz=nz),
        out_shape=[shape((comps * modes, half))] * 2,
        grid_spec=pltpu.PrefetchScalarGridSpec(
            num_scalar_prefetch=1,
            grid=(1,),
            in_specs=[pl.BlockSpec((modes * comps * nz, half), side)],
            out_specs=[pl.BlockSpec((comps * modes, half), lambda i, w: (0, 0))] * 2,
        ),
        compiler_params=params(16),
        cost_estimate=cost(modes * comps * nphi, 4 * modes * comps * nz * half),
        name="edge_layers",
    )(where, cot.reshape(modes * comps * nz, nphi))


def blanks(*like):
    return pl.pallas_call(
        lambda *outs: None,
        out_shape=[shape(dims, dtype) for dims, dtype in like],
        out_specs=[pl.BlockSpec(memory_space=pl.ANY)] * len(like),
        name="blanks",
    )()


def turn_kernel(where, cot, out, *, modes, nz, comps):
    for c in range(comps):
        for z in range(nz):
            out[c, z] = cot[pl.ds(c * nz + z, modes, stride=comps * nz), :].T


def turn_half(where, cot, foreign):
    modes, comps, nz, nphi = cot.shape
    half = nphi // 2
    side = (lambda i, w: (0, 1 - (w[0] >> 1))) if foreign else (lambda i, w: (0, w[0] >> 1))
    out = (comps, nz, half, modes)
    return pl.pallas_call(
        lambda *refs: turn_kernel(*refs, modes=modes, nz=nz, comps=comps),
        out_shape=shape(out),
        grid_spec=pltpu.PrefetchScalarGridSpec(
            num_scalar_prefetch=1,
            grid=(1,),
            in_specs=[pl.BlockSpec((modes * comps * nz, half), side)],
            out_specs=pl.BlockSpec(out, lambda i, w: (0, 0, 0, 0)),
        ),
        compiler_params=params(20),
        cost_estimate=cost(modes * comps * nz * half, 8 * modes * comps * nz * half),
        name="turn_half",
    )(where, cot.reshape(modes * comps * nz, nphi))


def first_kernel(turned, state, after, before, rate, *rest):
    outs, edges = rest[:-1], rest[-1]
    comps, nz, half, modes = turned.shape
    width = half // len(outs)
    for c in range(comps):
        edges[c, 0] = before[c * modes : (c + 1) * modes, :].T
        edges[c, 1] = after[c * modes : (c + 1) * modes, :].T
    turn = rotation_coeff * rate[...]
    step = 32
    for z in range(nz):
        for p in range(0, half, step):
            at = slice(p, p + step)
            st = state[z * half + p : z * half + p + step, :]
            cur = [turned[c, z, at, :] for c in range(comps)]
            others = (turn * cur[1], -turn * cur[0], None)
            for c in range(comps):
                upper = turned[c, z + 1, at, :] if z + 1 < nz else edges[c, 1, at, :]
                lower = turned[c, z - 1, at, :] if z else edges[c, 0, at, :]
                to = p % width
                outs[p // width][c, z, to : to + step, :] = stencil(cur[c], upper, lower, others[c], st)


def first_stencil(turned, state_turned, after, before, rate, chunks):
    comps, nz, half, modes = turned.shape
    out = (comps, nz, half // chunks, modes)
    return pl.pallas_call(
        first_kernel,
        out_shape=[shape(out)] * chunks,
        grid=(1,),
        in_specs=[
            pl.BlockSpec(turned.shape, lambda i: (0, 0, 0, 0)),
            pl.BlockSpec((nz * half, modes), lambda i: (0, 0)),
            pl.BlockSpec((comps * modes, half), lambda i: (0, 0)),
            pl.BlockSpec((comps * modes, half), lambda i: (0, 0)),
            pl.BlockSpec((1, modes), lambda i: (0, 0)),
        ],
        out_specs=[pl.BlockSpec(out, lambda i: (0, 0, 0, 0))] * chunks,
        scratch_shapes=[pltpu.VMEM((comps, 2, half, modes), F32)],
        compiler_params=params(32),
        cost_estimate=cost(12 * modes * comps * nz * half, 8 * modes * comps * nz * half),
        name="first_stencil",
    )(turned, state_turned, after, before, rate)


def helm_kernel(where, own, *refs):
    far, (high, low) = refs[:-2], refs[-2:]
    rows, modes = own.shape[1:]
    k = pl.program_id(0)
    wanted = block_of(k, where) ^ where[1]
    h, l = split(own[...])
    high[:, :, :modes] = h
    low[:, :, :modes] = l
    for d, ref in enumerate(far):

        @pl.when(wanted == d)
        def _(ref=ref):
            h, l = split(ref[...])
            high[:, :, modes:] = h
            low[:, :, modes:] = l


def block_of(k, where):
    return where[0] ^ (((k & 1) << 1) | (k >> 1))


def split_helm(where, own, far):
    comps, rows, modes = own.shape
    out = (comps, rows, 2 * modes)
    return pl.pallas_call(
        helm_kernel,
        out_shape=[shape(out, BF16)] * 2,
        grid_spec=pltpu.PrefetchScalarGridSpec(
            num_scalar_prefetch=1,
            grid=(rows // modes,),
            in_specs=[pl.BlockSpec((comps, modes, modes), lambda k, w: (0, block_of(k, w), 0))]
            + [pl.BlockSpec((comps, modes, modes), lambda k, w: (0, 0, 0))] * len(far),
            out_specs=[pl.BlockSpec((comps, modes, 2 * modes), lambda k, w: (0, k, 0))] * 2,
        ),
        compiler_params=params(16),
        cost_estimate=cost(4 * comps * rows * modes, 16 * comps * rows * modes),
        name="split_helm",
    )(where, own, *far)


def map1_kernel(own, far, own_peer, far_peer, high, low, out):
    _, nz, width, modes = own.shape
    parts = [ref[0].reshape(nz * width, modes) for ref in (own, far, own_peer, far_peer)]
    out[0] = product(parts, high[0], low[0]).reshape(nz, width, high.shape[2])


def map1(own, far, own_peer, far_peer, high, low, k):
    comps, nz, width, modes = far.shape
    rows, cols = high.shape[1:]
    here = pl.BlockSpec((1, nz, width, modes), lambda c: (c, 0, k, 0))
    group = pl.BlockSpec((1, nz, width, modes), lambda c: (c, 0, 0, 0))
    helm = pl.BlockSpec((1, rows, cols), lambda c: (c, 0, 0))
    return pl.pallas_call(
        map1_kernel,
        out_shape=shape((comps, nz, width, cols)),
        grid=(comps,),
        in_specs=[here, group, here, group, helm, helm],
        out_specs=pl.BlockSpec((1, nz, width, cols), lambda c: (c, 0, 0, 0)),
        compiler_params=params(24),
        cost_estimate=cost(6 * comps * nz * width * rows * cols, 4 * comps * (nz * width * (rows + cols) + rows * cols)),
        name=f"map1_{k}",
    )(own, far, own_peer, far_peer, high, low)


def layers1_kernel(*refs):
    firsts, lasts, (high, low, first, last) = refs[:4], refs[4:8], refs[8:]
    width = first.shape[1]
    parts = [jnp.concatenate([a[0, 0], b[0, 0]], axis=0) for a, b in zip(firsts, lasts)]
    res = product(parts, high[0], low[0])
    first[0] = res[:width]
    last[0] = res[width:]


def layers1(own, far, own_peer, far_peer, high, low, k):
    comps, nz, width, modes = far.shape
    rows, cols = high.shape[1:]
    block = (1, 1, width, modes)
    specs = []
    for z in (0, nz - 1):
        here = pl.BlockSpec(block, lambda c, z=z: (c, z, k, 0))
        group = pl.BlockSpec(block, lambda c, z=z: (c, z, 0, 0))
        specs += [here, group, here, group]
    helm = pl.BlockSpec((1, rows, cols), lambda c: (c, 0, 0))
    return pl.pallas_call(
        layers1_kernel,
        out_shape=[shape((comps, width, cols))] * 2,
        grid=(comps,),
        in_specs=[*specs, helm, helm],
        out_specs=[pl.BlockSpec((1, width, cols), lambda c: (c, 0, 0))] * 2,
        compiler_params=params(16),
        cost_estimate=cost(12 * comps * width * rows * cols, 4 * comps * (2 * width * (rows + cols) + rows * cols)),
        name=f"layers1_{k}",
    )(*[own, far, own_peer, far_peer] * 2, high, low)


def second_kernel(cur, after, before, state_own, state_far, rate, out, *, k, half):
    comps, nz, width, cols = cur.shape
    modes = cols // 2
    rates = (rate[...], state_far[nz * half : nz * half + 1, :])
    for g in range(2):
        lanes = slice(g * modes, (g + 1) * modes)
        turn = rotation_coeff * rates[g]
        state = (state_own, state_far)[g]
        for z in range(nz):
            st = state[z * half + k * width : z * half + (k + 1) * width, :]
            here = [cur[c, z, :, lanes] for c in range(comps)]
            others = (turn * here[1], -turn * here[0], None)
            for c in range(comps):
                upper = cur[c, z + 1, :, lanes] if z + 1 < nz else after[c, :, lanes]
                lower = cur[c, z - 1, :, lanes] if z else before[c, :, lanes]
                out[c, z, :, lanes] = stencil(here[c], upper, lower, others[c], st)


def second_stencil(cur, after, before, state_own, state_far, rate, k, half):
    return pl.pallas_call(
        lambda *refs: second_kernel(*refs, k=k, half=half),
        out_shape=shape(cur.shape),
        compiler_params=params(16),
        cost_estimate=cost(12 * cur.size, 8 * cur.size),
        name=f"second_stencil_{k}",
    )(cur, after, before, state_own, state_far, rate)


def map2_kernel(own, peer, high, low, out_own, *outs_far):
    _, nz, width, cols = own.shape
    parts = [ref[0].reshape(nz * width, cols) for ref in (own, peer)]
    res = product(parts, high[0], low[0]).reshape(nz, width, cols)
    out_own[0] = res[:, :, : cols // 2]
    per = pl.num_programs(0) // len(outs_far)
    for i, out in enumerate(outs_far):

        @pl.when(pl.program_id(0) // per == i)
        def _(out=out):
            out[0] = res[:, :, cols // 2 :]


def map2(own, peer, high, low, k, pieces):
    comps, nz, width, cols = own.shape
    rows, per = high.shape[1], comps // pieces
    chunk = pl.BlockSpec((1, nz, width, cols), lambda c: (c, 0, 0, 0))
    helm = pl.BlockSpec((1, rows, cols), lambda c: (c, 0, 0))
    block = (1, nz, width, cols // 2)
    far = [pl.BlockSpec(block, lambda c, i=i: (jnp.clip(c - i * per, 0, per - 1), 0, 0, 0)) for i in range(pieces)]
    return pl.pallas_call(
        map2_kernel,
        out_shape=[shape((comps, *block[1:]))] + [shape((per, *block[1:]))] * pieces,
        grid=(comps,),
        in_specs=[chunk, chunk, helm, helm],
        out_specs=[pl.BlockSpec(block, lambda c: (c, 0, 0, 0)), *far],
        compiler_params=params(24),
        cost_estimate=cost(6 * comps * nz * width * rows * cols, 4 * comps * (nz * width * (rows + cols) + rows * cols)),
        name=f"map2_{k}",
    )(own, peer, high, low)


def last_kernel(where, *refs, nz, chunks):
    ins, out = refs[:chunks], refs[-1]
    modes, _, width = out.shape
    rows = out.reshape(modes * nz, width)
    for z in range(nz):
        whole = jnp.concatenate([ref[0, z] for ref in ins], axis=0)
        rows[pl.ds(z, modes, stride=nz), :] = whole.T


def write_half(where, pieces, nphi, foreign, base=None, first=0):
    count = min(p.shape[0] for p in pieces)
    comps = max(p.shape[0] for p in pieces)
    nz, _, modes = pieces[0].shape[1:]
    chunks = len(pieces)
    side = (lambda w: 1 - (w[0] >> 1)) if foreign else (lambda w: w[0] >> 1)
    extra = () if base is None else (base,)

    def spec(piece):
        begin = first if piece.shape[0] > count else 0
        return pl.BlockSpec((1, *piece.shape[1:]), lambda c, w: (begin + c, 0, 0, 0))

    return pl.pallas_call(
        lambda *refs: last_kernel(*refs, nz=nz, chunks=chunks),
        out_shape=shape((modes, comps * nz, nphi)),
        grid_spec=pltpu.PrefetchScalarGridSpec(
            num_scalar_prefetch=1,
            grid=(count,),
            in_specs=[spec(p) for p in pieces] + [pl.BlockSpec(memory_space=pl.ANY)] * len(extra),
            out_specs=pl.BlockSpec((modes, nz, nphi // 2), lambda c, w: (0, first + c, side(w))),
        ),
        input_output_aliases={1 + chunks: 0} if extra else {},
        compiler_params=params(24),
        cost_estimate=cost(count * nz * modes * nphi, 4 * count * nz * modes * nphi),
        name=f"write_foreign_{first}" if foreign else "write_own",
    )(where, *pieces, *extra)


def tied(value, *others):
    return lax.optimization_barrier((value, *others))[0]


def on_device(cotangent, state_axial, helm_inverse, rotation_rate):
    modes, comps, nz, nphi = cotangent.shape
    half = nphi // 2
    peers, cols = lax.axis_size("rad"), lax.axis_size("col")
    up = [(i, (i + 1) % cols) for i in range(cols)]
    down = [(j, i) for i, j in up]

    def across(array):
        return lax.ppermute(array, "rad", [(i, i ^ 2) for i in range(peers)])

    def beside(array):
        return lax.ppermute(array, "rad", [(i, i ^ 1) for i in range(peers)])

    def hop(array, mask):
        return lax.ppermute(array, "col", [(i, i ^ mask) for i in range(cols)])

    lot = lax.axis_index("col").astype(jnp.int32) & (PIECES - 1)
    where = jnp.stack([lax.axis_index("rad").astype(jnp.int32), lot])
    rate = rotation_rate.reshape(1, modes)

    once = 1 + (where[0] >> 8)

    piece = across(lax.dynamic_slice_in_dim(helm_inverse, lot * modes, modes, axis=1))
    state_foreign = turn_state(where, state_axial, True, rate)
    state_far = across(state_foreign)

    def halos(leading, last):
        return lax.ppermute(leading, "col", down), lax.ppermute(last, "col", up)

    def foreign_half(step, _):
        here = where + (step >> 8)
        edges = halos(*edge_layers(here, cotangent, True))
        blocks = [tied(piece, here)]
        blocks += [hop(blocks[0], 1), hop(blocks[0], 2)]
        return (*first_stencil(turn_half(here, cotangent, True), state_foreign, *edges, rate, GROUPS), *blocks[1:])

    chunk = (comps, nz, half // GROUPS, modes)
    block = (comps, modes, modes)
    sent = lax.fori_loop(0, once, foreign_half, tuple(blanks(*[(chunk, F32)] * GROUPS, *[(block, F32)] * (PIECES - 2))))
    sent, blocks = sent[:GROUPS], [piece, *sent[GROUPS:]]
    far = [across(tied(s, state_far) if k else tied(s, piece)) for k, s in enumerate(sent)]

    def own_half(step, carry):
        here = where + (step >> 8)
        edges = halos(*edge_layers(here, entry, False))
        last_block = hop(tied(blocks[2], here), 1)
        edges = tuple(tied(e, last_block) for e in edges)
        state_own = turn_state(here, state_axial, False)
        (own,) = first_stencil(turn_half(here, entry, False), state_own, *edges, rate, 1)
        own_peer = beside(own)
        return (state_own, own, own_peer, *split_helm(here, helm_inverse, [*blocks, last_block]))

    entry = tied(cotangent, sent[0])
    columns = (comps, nz, half, modes)
    helm = (comps, peers * modes, 2 * modes)
    state_own, own, own_peer, high, low = lax.fori_loop(
        0, once, own_half, tuple(blanks(((nz * half, modes), F32), (columns, F32), (columns, F32), (helm, BF16), (helm, BF16)))
    )

    kept, back = [], []
    width = half // GROUPS
    for k in range(GROUPS):
        pieces = PIECES_BACK if k == GROUPS - 1 else 1

        def chain(step, _, k=k, pieces=pieces):
            here = tied(far[k], step)
            parts = (own, here, own_peer, beside(here), high, low)
            nxt = second_stencil(map1(*parts, k), *halos(*layers1(*parts, k)), state_own, state_far, rate, k, half)
            return tuple(map2(nxt, beside(nxt), high, low, k, pieces))

        spare = tied(sent[k], kept[-1]) if kept else sent[k]
        parts = blanks(*[((comps // pieces, nz, width, modes), F32)] * pieces)
        mine, *theirs = lax.fori_loop(0, once, chain, (spare, *parts))
        kept.append(mine)
        back.append([across(t) for t in theirs])
    out = write_half(where, kept, nphi, False)
    for i in range(PIECES_BACK):
        group = [b[0] if len(b) == 1 else b[i] for b in back]
        out = write_half(where, group, nphi, True, out, i * (comps // PIECES_BACK))
    return out.reshape(modes, comps, nz, nphi)


def solution(mesh):
    in_specs = (P("rad", None, "col", None), P("rad", "col", None), P(None, None, "rad"), P("rad"))
    out_specs = P("rad", None, "col", None)
    return jax.shard_map(
        on_device, mesh=mesh, in_specs=in_specs, out_specs=out_specs, check_vma=False
    )
```

```python
import jax
import jax.numpy as jnp
from jax import lax
from jax.experimental import pallas as pl
from jax.experimental.pallas import tpu as pltpu
from jax.sharding import PartitionSpec as P

SECTIONS = 2
GROUPS = 2
PIECES_BACK = 6
RATE_ROWS = 8
PIECES = 4

diffusion_coeff = 0.2
advection_coeff = 0.15
rotation_coeff = 0.25

F32 = jnp.float32
BF16 = jnp.bfloat16
MB = 1 << 20


def shape(dims, dtype=F32):
    return jax.ShapeDtypeStruct(dims, dtype)


def cost(flops, moved):
    return pl.CostEstimate(flops=int(flops), bytes_accessed=int(moved), transcendentals=0)


def params(limit=40):
    return pltpu.CompilerParams(vmem_limit_bytes=limit * MB)


def stencil(cur, upper, lower, other, state):
    up = diffusion_coeff - advection_coeff * state
    down = diffusion_coeff + advection_coeff * state
    out = (1.0 - 2.0 * diffusion_coeff) * cur + up * upper + down * lower
    return out if other is None else out + other


def split(values):
    high = values.astype(BF16)
    return high, (values - high.astype(F32)).astype(BF16)


def product(x_parts, h_high, h_low):
    pairs = [split(x) for x in x_parts]
    high = jnp.concatenate([p[0] for p in pairs], axis=1)
    low = jnp.concatenate([p[1] for p in pairs], axis=1)

    def dot(a, b):
        return jnp.dot(a, b, preferred_element_type=F32)

    return dot(high, h_high) + (dot(high, h_low) + dot(low, h_high))


def state_kernel(where, state, *refs, modes, nz):
    out = refs[-1]
    width = state.shape[1]
    rows = nz * width
    for z in range(nz):
        out[z * width : (z + 1) * width, :] = state[pl.ds(z, modes, stride=nz), :].T
    if len(refs) > 1:
        out[rows:, :] = jnp.broadcast_to(refs[0][...], (RATE_ROWS, modes))


def turn_state(where, state, foreign, rate=None):
    modes, nz, nphi = state.shape
    half = nphi // 2
    side = (lambda i, w: (0, 1 - (w[0] >> 1))) if foreign else (lambda i, w: (0, w[0] >> 1))
    rows, more, more_specs = nz * half, (), []
    if rate is not None:
        rows += RATE_ROWS
        more = (rate,)
        more_specs = [pl.BlockSpec((1, modes), lambda i, w: (0, 0))]
    return pl.pallas_call(
        lambda *refs: state_kernel(*refs, modes=modes, nz=nz),
        out_shape=shape((rows, modes)),
        grid_spec=pltpu.PrefetchScalarGridSpec(
            num_scalar_prefetch=1,
            grid=(1,),
            in_specs=[pl.BlockSpec((modes * nz, half), side)] + more_specs,
            out_specs=pl.BlockSpec((rows, modes), lambda i, w: (0, 0)),
        ),
        compiler_params=params(16),
        cost_estimate=cost(rows * modes, 8 * rows * modes),
        name="turn_state",
    )(where, state.reshape(modes * nz, nphi), *more)


def edge_kernel(where, cot, leading, last, *, modes, nz):
    for c in range(3):
        at = slice(c * modes, (c + 1) * modes)
        leading[at, :] = cot[pl.ds(c * nz, modes, stride=3 * nz), :]
        last[at, :] = cot[pl.ds(c * nz + nz - 1, modes, stride=3 * nz), :]


def edge_layers(where, cot, foreign):
    modes, comps, nz, nphi = cot.shape
    half = nphi // 2
    side = (lambda i, w: (0, 1 - (w[0] >> 1))) if foreign else (lambda i, w: (0, w[0] >> 1))
    return pl.pallas_call(
        lambda *refs: edge_kernel(*refs, modes=modes, nz=nz),
        out_shape=[shape((comps * modes, half))] * 2,
        grid_spec=pltpu.PrefetchScalarGridSpec(
            num_scalar_prefetch=1,
            grid=(1,),
            in_specs=[pl.BlockSpec((modes * comps * nz, half), side)],
            out_specs=[pl.BlockSpec((comps * modes, half), lambda i, w: (0, 0))] * 2,
        ),
        compiler_params=params(16),
        cost_estimate=cost(modes * comps * nphi, 4 * modes * comps * nz * half),
        name="edge_layers",
    )(where, cot.reshape(modes * comps * nz, nphi))


def blanks(*like):
    return pl.pallas_call(
        lambda *outs: None,
        out_shape=[shape(dims, dtype) for dims, dtype in like],
        out_specs=[pl.BlockSpec(memory_space=pl.ANY)] * len(like),
        name="blanks",
    )()


def turn_kernel(where, cot, out, *, modes, nz, comps):
    for c in range(comps):
        for z in range(nz):
            out[c, z] = cot[pl.ds(c * nz + z, modes, stride=comps * nz), :].T


def turn_half(where, cot, foreign):
    modes, comps, nz, nphi = cot.shape
    half = nphi // 2
    side = (lambda i, w: (0, 1 - (w[0] >> 1))) if foreign else (lambda i, w: (0, w[0] >> 1))
    out = (comps, nz, half, modes)
    return pl.pallas_call(
        lambda *refs: turn_kernel(*refs, modes=modes, nz=nz, comps=comps),
        out_shape=shape(out),
        grid_spec=pltpu.PrefetchScalarGridSpec(
            num_scalar_prefetch=1,
            grid=(1,),
            in_specs=[pl.BlockSpec((modes * comps * nz, half), side)],
            out_specs=pl.BlockSpec(out, lambda i, w: (0, 0, 0, 0)),
        ),
        compiler_params=params(20),
        cost_estimate=cost(modes * comps * nz * half, 8 * modes * comps * nz * half),
        name="turn_half",
    )(where, cot.reshape(modes * comps * nz, nphi))


def first_kernel(turned, state, after, before, rate, *rest):
    outs, edges = rest[:-1], rest[-1]
    comps, nz, half, modes = turned.shape
    width = half // len(outs)
    for c in range(comps):
        edges[c, 0] = before[c * modes : (c + 1) * modes, :].T
        edges[c, 1] = after[c * modes : (c + 1) * modes, :].T
    turn = rotation_coeff * rate[...]
    step = 32
    for z in range(nz):
        for p in range(0, half, step):
            at = slice(p, p + step)
            st = state[z * half + p : z * half + p + step, :]
            cur = [turned[c, z, at, :] for c in range(comps)]
            others = (turn * cur[1], -turn * cur[0], None)
            for c in range(comps):
                upper = turned[c, z + 1, at, :] if z + 1 < nz else edges[c, 1, at, :]
                lower = turned[c, z - 1, at, :] if z else edges[c, 0, at, :]
                to = p % width
                outs[p // width][c, z, to : to + step, :] = stencil(cur[c], upper, lower, others[c], st)


def first_stencil(turned, state_turned, after, before, rate, chunks):
    comps, nz, half, modes = turned.shape
    out = (comps, nz, half // chunks, modes)
    return pl.pallas_call(
        first_kernel,
        out_shape=[shape(out)] * chunks,
        grid=(1,),
        in_specs=[
            pl.BlockSpec(turned.shape, lambda i: (0, 0, 0, 0)),
            pl.BlockSpec((nz * half, modes), lambda i: (0, 0)),
            pl.BlockSpec((comps * modes, half), lambda i: (0, 0)),
            pl.BlockSpec((comps * modes, half), lambda i: (0, 0)),
            pl.BlockSpec((1, modes), lambda i: (0, 0)),
        ],
        out_specs=[pl.BlockSpec(out, lambda i: (0, 0, 0, 0))] * chunks,
        scratch_shapes=[pltpu.VMEM((comps, 2, half, modes), F32)],
        compiler_params=params(32),
        cost_estimate=cost(12 * modes * comps * nz * half, 8 * modes * comps * nz * half),
        name="first_stencil",
    )(turned, state_turned, after, before, rate)


def helm_kernel(where, own, *refs):
    far, (high, low) = refs[:-2], refs[-2:]
    rows, modes = own.shape[1:]
    k = pl.program_id(0)
    wanted = block_of(k, where) ^ where[1]
    h, l = split(own[...])
    high[:, :, :modes] = h
    low[:, :, :modes] = l
    for d, ref in enumerate(far):

        @pl.when(wanted == d)
        def _(ref=ref):
            h, l = split(ref[...])
            high[:, :, modes:] = h
            low[:, :, modes:] = l


def block_of(k, where):
    return where[0] ^ (((k & 1) << 1) | (k >> 1))


def split_helm(where, own, far):
    comps, rows, modes = own.shape
    out = (comps, rows, 2 * modes)
    return pl.pallas_call(
        helm_kernel,
        out_shape=[shape(out, BF16)] * 2,
        grid_spec=pltpu.PrefetchScalarGridSpec(
            num_scalar_prefetch=1,
            grid=(rows // modes,),
            in_specs=[pl.BlockSpec((comps, modes, modes), lambda k, w: (0, block_of(k, w), 0))]
            + [pl.BlockSpec((comps, modes, modes), lambda k, w: (0, 0, 0))] * len(far),
            out_specs=[pl.BlockSpec((comps, modes, 2 * modes), lambda k, w: (0, k, 0))] * 2,
        ),
        compiler_params=params(16),
        cost_estimate=cost(4 * comps * rows * modes, 16 * comps * rows * modes),
        name="split_helm",
    )(where, own, *far)


def map1_kernel(own, far, own_peer, far_peer, high, low, out):
    _, nz, width, modes = own.shape
    parts = [ref[0].reshape(nz * width, modes) for ref in (own, far, own_peer, far_peer)]
    out[0] = product(parts, high[0], low[0]).reshape(nz, width, high.shape[2])


def map1(own, far, own_peer, far_peer, high, low, k):
    comps, nz, width, modes = far.shape
    rows, cols = high.shape[1:]
    here = pl.BlockSpec((1, nz, width, modes), lambda c: (c, 0, k, 0))
    group = pl.BlockSpec((1, nz, width, modes), lambda c: (c, 0, 0, 0))
    helm = pl.BlockSpec((1, rows, cols), lambda c: (c, 0, 0))
    return pl.pallas_call(
        map1_kernel,
        out_shape=shape((comps, nz, width, cols)),
        grid=(comps,),
        in_specs=[here, group, here, group, helm, helm],
        out_specs=pl.BlockSpec((1, nz, width, cols), lambda c: (c, 0, 0, 0)),
        compiler_params=params(24),
        cost_estimate=cost(6 * comps * nz * width * rows * cols, 4 * comps * (nz * width * (rows + cols) + rows * cols)),
        name=f"map1_{k}",
    )(own, far, own_peer, far_peer, high, low)


def layers1_kernel(*refs):
    firsts, lasts, (high, low, first, last) = refs[:4], refs[4:8], refs[8:]
    width = first.shape[1]
    parts = [jnp.concatenate([a[0, 0], b[0, 0]], axis=0) for a, b in zip(firsts, lasts)]
    res = product(parts, high[0], low[0])
    first[0] = res[:width]
    last[0] = res[width:]


def layers1(own, far, own_peer, far_peer, high, low, k):
    comps, nz, width, modes = far.shape
    rows, cols = high.shape[1:]
    block = (1, 1, width, modes)
    specs = []
    for z in (0, nz - 1):
        here = pl.BlockSpec(block, lambda c, z=z: (c, z, k, 0))
        group = pl.BlockSpec(block, lambda c, z=z: (c, z, 0, 0))
        specs += [here, group, here, group]
    helm = pl.BlockSpec((1, rows, cols), lambda c: (c, 0, 0))
    return pl.pallas_call(
        layers1_kernel,
        out_shape=[shape((comps, width, cols))] * 2,
        grid=(comps,),
        in_specs=[*specs, helm, helm],
        out_specs=[pl.BlockSpec((1, width, cols), lambda c: (c, 0, 0))] * 2,
        compiler_params=params(16),
        cost_estimate=cost(12 * comps * width * rows * cols, 4 * comps * (2 * width * (rows + cols) + rows * cols)),
        name=f"layers1_{k}",
    )(*[own, far, own_peer, far_peer] * 2, high, low)


def second_kernel(cur, after, before, state_own, state_far, rate, out, *, k, half):
    comps, nz, width, cols = cur.shape
    modes = cols // 2
    rates = (rate[...], state_far[nz * half : nz * half + 1, :])
    for g in range(2):
        lanes = slice(g * modes, (g + 1) * modes)
        turn = rotation_coeff * rates[g]
        state = (state_own, state_far)[g]
        for z in range(nz):
            st = state[z * half + k * width : z * half + (k + 1) * width, :]
            here = [cur[c, z, :, lanes] for c in range(comps)]
            others = (turn * here[1], -turn * here[0], None)
            for c in range(comps):
                upper = cur[c, z + 1, :, lanes] if z + 1 < nz else after[c, :, lanes]
                lower = cur[c, z - 1, :, lanes] if z else before[c, :, lanes]
                out[c, z, :, lanes] = stencil(here[c], upper, lower, others[c], st)


def second_stencil(cur, after, before, state_own, state_far, rate, k, half):
    return pl.pallas_call(
        lambda *refs: second_kernel(*refs, k=k, half=half),
        out_shape=shape(cur.shape),
        compiler_params=params(16),
        cost_estimate=cost(12 * cur.size, 8 * cur.size),
        name=f"second_stencil_{k}",
    )(cur, after, before, state_own, state_far, rate)


def map2_kernel(own, peer, high, low, out_own, *outs_far):
    _, nz, width, cols = own.shape
    parts = [ref[0].reshape(nz * width, cols) for ref in (own, peer)]
    res = product(parts, high[0], low[0]).reshape(nz, width, cols)
    out_own[0] = res[:, :, : cols // 2]
    if len(outs_far) == 1:
        outs_far[0][0] = res[:, :, cols // 2 :]
        return
    deep = outs_far[0].shape[1]
    cuts = nz // deep
    for i, out in enumerate(outs_far):

        @pl.when(pl.program_id(0) == i // cuts)
        def _(out=out, z=i % cuts * deep):
            out[0] = res[z : z + deep, :, cols // 2 :]


def map2(own, peer, high, low, k, pieces):
    comps, nz, width, cols = own.shape
    rows = high.shape[1]
    chunk = pl.BlockSpec((1, nz, width, cols), lambda c: (c, 0, 0, 0))
    helm = pl.BlockSpec((1, rows, cols), lambda c: (c, 0, 0))
    block = (1, nz, width, cols // 2)
    far = [pl.BlockSpec(block, lambda c: (c, 0, 0, 0))]
    far_shapes = [shape((comps, *block[1:]))]
    if pieces > 1:
        part = (1, nz * comps // pieces, width, cols // 2)
        far, far_shapes = [pl.BlockSpec(part, lambda c: (0, 0, 0, 0))] * pieces, [shape(part)] * pieces
    return pl.pallas_call(
        map2_kernel,
        out_shape=[shape((comps, *block[1:])), *far_shapes],
        grid=(comps,),
        in_specs=[chunk, chunk, helm, helm],
        out_specs=[pl.BlockSpec(block, lambda c: (c, 0, 0, 0)), *far],
        compiler_params=params(24),
        cost_estimate=cost(6 * comps * nz * width * rows * cols, 4 * comps * (nz * width * (rows + cols) + rows * cols)),
        name=f"map2_{k}",
    )(own, peer, high, low)


def last_kernel(where, *refs, nz, chunks):
    ins, out = refs[:chunks], refs[-1]
    modes, _, width = out.shape
    rows = out.reshape(modes * nz, width)
    for z in range(nz):
        whole = jnp.concatenate([ref[0, z] for ref in ins], axis=0)
        rows[pl.ds(z, modes, stride=nz), :] = whole.T


def write_half(where, pieces, comps, nz, nphi, foreign, base=None, first=0):
    deep = min(p.shape[1] for p in pieces)
    cuts = nz // deep
    count = min(p.shape[0] for p in pieces)
    modes = pieces[0].shape[3]
    chunks = len(pieces)
    side = (lambda w: 1 - (w[0] >> 1)) if foreign else (lambda w: w[0] >> 1)
    extra = () if base is None else (base,)

    def spec(piece):
        at = first if piece.shape[1] > deep else 0
        return pl.BlockSpec((1, deep, *piece.shape[2:]), lambda c, w: (c + at // cuts, at % cuts, 0, 0))

    return pl.pallas_call(
        lambda *refs: last_kernel(*refs, nz=deep, chunks=chunks),
        out_shape=shape((modes, comps * nz, nphi)),
        grid_spec=pltpu.PrefetchScalarGridSpec(
            num_scalar_prefetch=1,
            grid=(count,),
            in_specs=[spec(p) for p in pieces] + [pl.BlockSpec(memory_space=pl.ANY)] * len(extra),
            out_specs=pl.BlockSpec((modes, deep, nphi // 2), lambda c, w: (0, first + c, side(w))),
        ),
        input_output_aliases={1 + chunks: 0} if extra else {},
        compiler_params=params(24),
        cost_estimate=cost(count * deep * modes * nphi, 4 * count * deep * modes * nphi),
        name=f"write_foreign_{first}" if foreign else "write_own",
    )(where, *pieces, *extra)


def tied(value, *others):
    return lax.optimization_barrier((value, *others))[0]


def on_device(cotangent, state_axial, helm_inverse, rotation_rate):
    modes, comps, nz, nphi = cotangent.shape
    half = nphi // 2
    peers, cols = lax.axis_size("rad"), lax.axis_size("col")
    up = [(i, (i + 1) % cols) for i in range(cols)]
    down = [(j, i) for i, j in up]

    def across(array):
        return lax.ppermute(array, "rad", [(i, i ^ 2) for i in range(peers)])

    def beside(array):
        return lax.ppermute(array, "rad", [(i, i ^ 1) for i in range(peers)])

    def hop(array, mask):
        return lax.ppermute(array, "col", [(i, i ^ mask) for i in range(cols)])

    lot = lax.axis_index("col").astype(jnp.int32) & (PIECES - 1)
    where = jnp.stack([lax.axis_index("rad").astype(jnp.int32), lot])
    rate = rotation_rate.reshape(1, modes)

    once = 1 + (where[0] >> 8)

    piece = across(lax.dynamic_slice_in_dim(helm_inverse, lot * modes, modes, axis=1))
    state_foreign = turn_state(where, state_axial, True, rate)
    state_far = across(state_foreign)

    def halos(leading, last):
        return lax.ppermute(leading, "col", down), lax.ppermute(last, "col", up)

    def foreign_half(step, _):
        here = where + (step >> 8)
        edges = halos(*edge_layers(here, cotangent, True))
        blocks = [tied(piece, here)]
        blocks += [hop(blocks[0], 1), hop(blocks[0], 2)]
        return (*first_stencil(turn_half(here, cotangent, True), state_foreign, *edges, rate, GROUPS), *blocks[1:])

    chunk = (comps, nz, half // GROUPS, modes)
    block = (comps, modes, modes)
    sent = lax.fori_loop(0, once, foreign_half, tuple(blanks(*[(chunk, F32)] * GROUPS, *[(block, F32)] * (PIECES - 2))))
    sent, blocks = sent[:GROUPS], [piece, *sent[GROUPS:]]
    far = [across(tied(s, state_far) if k else tied(s, piece)) for k, s in enumerate(sent)]

    def own_half(step, carry):
        here = where + (step >> 8)
        edges = halos(*edge_layers(here, entry, False))
        last_block = hop(tied(blocks[2], here), 1)
        edges = tuple(tied(e, last_block) for e in edges)
        state_own = turn_state(here, state_axial, False)
        (own,) = first_stencil(turn_half(here, entry, False), state_own, *edges, rate, 1)
        own_peer = beside(own)
        return (state_own, own, own_peer, *split_helm(here, helm_inverse, [*blocks, last_block]))

    entry = tied(cotangent, sent[0])
    columns = (comps, nz, half, modes)
    helm = (comps, peers * modes, 2 * modes)
    state_own, own, own_peer, high, low = lax.fori_loop(
        0, once, own_half, tuple(blanks(((nz * half, modes), F32), (columns, F32), (columns, F32), (helm, BF16), (helm, BF16)))
    )

    kept, back = [], []
    width = half // GROUPS
    for k in range(GROUPS):
        pieces = PIECES_BACK if k == GROUPS - 1 else 1

        def chain(step, _, k=k, pieces=pieces):
            here = tied(far[k], step)
            parts = (own, here, own_peer, beside(here), high, low)
            nxt = second_stencil(map1(*parts, k), *halos(*layers1(*parts, k)), state_own, state_far, rate, k, half)
            return tuple(map2(nxt, beside(nxt), high, low, k, pieces))

        spare = tied(sent[k], kept[-1]) if kept else sent[k]
        part = (comps, nz, width, modes) if pieces == 1 else (1, nz * comps // pieces, width, modes)
        parts = blanks(*[(part, F32)] * pieces)
        mine, *theirs = lax.fori_loop(0, once, chain, (spare, *parts))
        kept.append(mine)
        back.append([across(t) for t in theirs])
    out = write_half(where, kept, comps, nz, nphi, False)
    for i in range(PIECES_BACK):
        group = [b[0] if len(b) == 1 else b[i] for b in back]
        out = write_half(where, group, comps, nz, nphi, True, out, i)
    return out.reshape(modes, comps, nz, nphi)


def solution(mesh):
    in_specs = (P("rad", None, "col", None), P("rad", "col", None), P(None, None, "rad"), P("rad"))
    out_specs = P("rad", None, "col", None)
    return jax.shard_map(
        on_device, mesh=mesh, in_specs=in_specs, out_specs=out_specs, check_vma=False
    )
```
